256 devices in a mesh: mode: 16 (over z, core), dom: 16 (over y, x).
Axes of the slice: x: 4, y: 4, z: 8, core: 2. Of those that a mesh axis runs over, the one named last changes fastest.
Arguments:
- velocity: float32 [3, 128, 2, 32768], P(None, 'mode', None, 'dom'), may hold values from -0.375 to 0.375
- vorticity: float32 [3, 128, 2, 32768], P(None, 'mode', None, 'dom'), may hold values from -0.375 to 0.375
- blocks: float32 [9, 64, 64], replicated, may hold values from -0.042 to 0.042
- nbr_ref: int32 [9, 512], P(None, 'dom'), may hold values from 0 to 47
- send_list: int32 [2, 128], P(None, 'dom'), may hold values from 0 to 31
Outputs:
- velocity_new: float32 [3, 128, 2, 32768], P(None, 'mode', None, 'dom')
The draws below stay inside these ranges and needn't reach their ends.
Inputs may be any that keep to these rules, and one draw needn't show every extreme that they name: nbr_ref indexes the extended list of the element's own partition; partitions form a cycle. send_list holds local element numbers of the partition that holds the entry.
All inputs are finite; a program needn't handle non-finite values.
Results may differ from the reference program's by a relative error of at most 0.0001.
Values sent between devices are 32-bit elements; how exact they have to be, the bound alone decides.
No kernel may reach another device: no remote copies, remote signals or barrier semaphores. Data moves between devices by JAX's collectives and lax.ppermute only.
A program may use at most 64 MiB of HBM per device.

```python
import jax
import jax.numpy as jnp
from jax import lax

NP = 64
MODES = 128
NBR = 9
CHEB = 4
ELEM_DEV = 32
SEND = 8
ELEMS = 512
N_DOM = 16


def plant(values, key, low, top_value):
    index_at = [jax.random.randint(jax.random.fold_in(key, axis), (), 0, length) for axis, length in enumerate(values.shape)]
    widest = values.shape.index(max(values.shape))
    neighbour = index_at[:widest] + [(index_at[widest] + 1) % values.shape[widest]] + index_at[widest + 1:]
    return values.at[tuple(index_at)].set(low).at[tuple(neighbour)].set(top_value)


def block_scale(own_key, shape, split, low, high):
    def one(axis_at, shards_of):
        steps = jax.random.uniform(jax.random.fold_in(jax.random.fold_in(own_key, 6), axis_at), (shards_of,), jnp.float32, low / len(split), high / len(split))
        return jnp.repeat(jnp.exp(steps), shape[axis_at] // shards_of).reshape((-1,) + (1,) * (len(shape) - axis_at - 1))

    gain = one(*split[0])
    for cut in split[1:]:
        gain = gain * one(*cut)
    return gain


def normal_values(rng, dims, deviation, bound, split=(), held_as=jnp.bfloat16):
    drawn = deviation * jax.random.normal(rng, dims, jnp.float32)
    if split:
        drawn = drawn * block_scale(rng, dims, split, -0.22, 0.18)
    return jnp.clip(drawn, -bound, bound).astype(held_as)


def setup_inputs(seed: int = 0) -> dict:
    arg_keys = jax.random.split(jax.random.key(seed), 6)
    velocity = normal_values(arg_keys[0], (3, MODES, 2, ELEMS * NP), (1.0 / (2 * MODES) ** 0.5), 0.375, ((1, 16), (3, 16)), jnp.float32)
    vorticity = normal_values(arg_keys[1], (3, MODES, 2, ELEMS * NP), (1.0 / (2 * MODES) ** 0.5), 0.375, ((1, 16), (3, 16)), jnp.float32)
    blocks = normal_values(arg_keys[2], (NBR, NP, NP), (0.056 / NP ** 0.5), 0.042, (), jnp.float32)
    nbr_ref = plant(jax.random.randint(arg_keys[3], (NBR, ELEMS), 0, ELEM_DEV + 2 * SEND), jax.random.fold_in(arg_keys[3], 1), 0, (ELEM_DEV + 2 * SEND) - 1).astype(jnp.int32)
    send_list = plant(jax.random.randint(arg_keys[4], (2, N_DOM * SEND), 0, ELEM_DEV), jax.random.fold_in(arg_keys[4], 1), 0, ELEM_DEV - 1).astype(jnp.int32)
    return {"velocity": velocity, "vorticity": vorticity, "blocks": blocks, "nbr_ref": nbr_ref, "send_list": send_list}


def spanwise_tables(count):
    mode_ids = jnp.arange(count, dtype=jnp.int32)
    planes = jnp.arange(2 * count, dtype=jnp.int32)
    phase = (planes[:, None] * mode_ids[None, :]) % (2 * count)
    angle = (2.0 * jnp.pi / (2 * count)) * phase.astype(jnp.float32)
    weights = jnp.where(mode_ids == 0, 1.0, 2.0).astype(jnp.float32)
    inv_cos = weights[None, :] * jnp.cos(angle)
    inv_sin = weights[None, :] * jnp.sin(angle)
    back_cos = jnp.cos(angle).T / (2 * count)
    back_sin = -jnp.sin(angle).T / (2 * count)
    return inv_cos, inv_sin, back_cos, back_sin


def line_forcing(vel_lines, vort_lines, tables):
    inv_cos, inv_sin, back_cos, back_sin = tables
    highest = lax.Precision.HIGHEST

    def to_planes(field):
        return (jnp.einsum('zk,ckx->czx', inv_cos, field[:, :, 0], precision=highest)
                - jnp.einsum('zk,ckx->czx', inv_sin, field[:, :, 1], precision=highest))

    vel_planes = to_planes(vel_lines)
    vort_planes = to_planes(vort_lines)
    cross = jnp.stack([
        vel_planes[1] * vort_planes[2] - vel_planes[2] * vort_planes[1],
        vel_planes[2] * vort_planes[0] - vel_planes[0] * vort_planes[2],
        vel_planes[0] * vort_planes[1] - vel_planes[1] * vort_planes[0]])
    real_part = jnp.einsum('kz,czx->ckx', back_cos, cross, precision=highest)
    imag_part = jnp.einsum('kz,czx->ckx', back_sin, cross, precision=highest)
    return jnp.stack([real_part, imag_part], axis=2)


def unmerge(field):
    return jnp.swapaxes(field.reshape(3, MODES, 2, ELEMS, NP), 3, 4)


def remerge(field):
    return jnp.swapaxes(field, 3, 4).reshape(3, MODES, 2, ELEMS * NP)


def reference(velocity, vorticity, blocks, nbr_ref, send_list):
    highest = lax.Precision.HIGHEST
    tables = spanwise_tables(MODES)
    velocity = unmerge(velocity)
    vorticity = unmerge(vorticity)

    def one_point(pair):
        return line_forcing(pair[0], pair[1], tables)

    forcing = lax.map(one_point, (jnp.moveaxis(velocity, 3, 0), jnp.moveaxis(vorticity, 3, 0)))
    forcing = jnp.moveaxis(forcing, 0, 3)
    wavenum = jnp.arange(MODES, dtype=jnp.int32).astype(jnp.float32) / MODES
    inv_diag = (1.0 / (1.0 + 4.0 * wavenum * wavenum)).reshape(1, MODES, 1, 1, 1)
    element = jnp.arange(ELEMS, dtype=jnp.int32)
    partition = jnp.broadcast_to(element // ELEM_DEV, nbr_ref.shape)
    below = (partition - 1) % N_DOM
    above = (partition + 1) % N_DOM
    off_below = jnp.clip(nbr_ref - ELEM_DEV, 0, SEND - 1)
    off_above = jnp.clip(nbr_ref - ELEM_DEV - SEND, 0, SEND - 1)
    from_below = below * ELEM_DEV + send_list[0][below * SEND + off_below]
    from_above = above * ELEM_DEV + send_list[1][above * SEND + off_above]
    global_ids = jnp.where(nbr_ref < ELEM_DEV, partition * ELEM_DEV + nbr_ref,
                           jnp.where(nbr_ref < ELEM_DEV + SEND, from_below, from_above)).astype(jnp.int32)

    def apply_operator(field):
        total = jnp.zeros_like(field)
        for slot in range(blocks.shape[0]):
            picked = jnp.take(field, global_ids[slot], axis=4)
            total = total + jnp.einsum('pq,cmrqe->cmrpe', blocks[slot], picked, precision=highest)
        return field + inv_diag * total

    rhs = (velocity + forcing) * inv_diag
    solution = jnp.zeros_like(rhs)
    resid = rhs
    direction = rhs
    rho = 0.5
    for step in range(CHEB):
        solution = solution + direction
        resid = resid - apply_operator(direction)
        rho_next = 1.0 / (4.0 - rho)
        direction = (rho_next * rho) * direction + (4.0 * rho_next) * resid
        rho = rho_next
    return remerge(solution + direction)
```

```python
import functools

import jax
import jax.numpy as jnp
import numpy as np
from jax import lax
from jax.experimental import pallas as pl
from jax.experimental.pallas import tpu as pltpu
from jax.sharding import PartitionSpec as P

CHEB = 4
NP = 64
COMPS = 3
LANES = 128
bf16, f32 = jnp.bfloat16, jnp.float32


def split(value):
    high = value.astype(bf16)
    return high, (value - high.astype(f32)).astype(bf16)


def np_split(value):
    high = value.astype(np.float32).astype(bf16)
    return high, (value - high.astype(np.float64)).astype(np.float32).astype(bf16)


def spanwise_tables(count):
    planes = 2 * count
    angle = 2 * np.pi / planes * ((np.arange(planes)[:, None] * np.arange(count)[None, :]) % planes)
    weights = np.where(np.arange(count) == 0, 1.0, 2.0)
    forward = np.stack([weights * np.cos(angle), -weights * np.sin(angle)], axis=2).reshape(planes, planes)
    back = np.stack([np.cos(angle).T, -np.sin(angle).T], axis=1).reshape(planes, planes) / planes
    return np_split(forward) + np_split(back)


def dot(a, b):
    return jnp.dot(a, b, preferred_element_type=f32)


def dot3(a, b):
    return dot(a[0], b[0]) + dot(a[1], b[0]) + dot(a[0], b[1])


def lines_kernel(lines, table, fwd_hi, fwd_lo, back_hi, back_lo, out):
    senders, rows, _ = lines.shape
    per = rows // (2 * COMPS)
    count = senders * per
    fields = [lines[:, i * per:(i + 1) * per, :].reshape(count, LANES) for i in range(2 * COMPS)]
    forward = (fwd_hi[...], fwd_lo[...])
    planes = [dot3(forward, split(jnp.concatenate(fields[i:i + 2], axis=1))) for i in range(0, 2 * COMPS, 2)]
    planes = [half for pair in planes for half in (pair[:, :LANES], pair[:, LANES:])]
    u, w = planes[:COMPS], planes[COMPS:]
    cross = jnp.concatenate([u[(c + 1) % 3] * w[(c + 2) % 3] - u[(c + 2) % 3] * w[(c + 1) % 3] for c in range(3)], axis=1)
    forcing = dot3((back_hi[...], back_lo[...]), split(cross))
    mode = lax.broadcasted_iota(jnp.int32, (count, LANES), 0) >> 1
    wavenum = mode.astype(f32) * (2.0 / count)
    inv_diag = 1.0 / (1.0 + 4.0 * wavenum * wavenum)
    for c in range(COMPS):
        out[:, 0, c * LANES:(c + 1) * LANES] = (fields[c] + forcing[:, c * LANES:(c + 1) * LANES]) * inv_diag
    out[:, 0, COMPS * LANES:] = jnp.broadcast_to(table[...], (count, LANES))


def solve_kernel(parts, pairs, slots, send, scal, state_in, w_hi, w_lo, out,
                 onehot, ext_hi, ext_lo, y_hi, y_lo, sol, resid, dirn, kap):
    elems = 2 * pairs
    half = lax.broadcasted_iota(jnp.int32, (parts * pairs, LANES), 1) < NP
    x = [state_in[:, c * LANES:(c + 1) * LANES] for c in range(COMPS)]
    swap = [pltpu.roll(v, NP, 1) for v in x]
    shape = (parts, pairs, LANES)
    zero = jnp.zeros_like(x[0])
    dirn[:, 0, :, :LANES] = jnp.where(half, x[0], swap[1]).reshape(shape)
    dirn[:, 0, :, LANES:] = jnp.where(half, x[2], zero).reshape(shape)
    dirn[:, 1, :, :LANES] = jnp.where(half, swap[0], x[1]).reshape(shape)
    dirn[:, 1, :, LANES:] = jnp.where(half, swap[2], zero).reshape(shape)
    resid[...] = dirn[...]
    sol[...] = jnp.zeros_like(sol)

    refs = state_in[:, COMPS * LANES:]
    below = jnp.concatenate([refs[-pairs:], refs[:-pairs]], axis=0)
    above = jnp.concatenate([refs[pairs:], refs[:pairs]], axis=0)
    local = refs
    first = 2 * slots
    for s in range(send):
        local = jnp.where(refs == float(elems + s), below[:, first + s:first + s + 1], local)
        at = first + send + s
        local = jnp.where(refs == float(elems + send + s), above[:, at:at + 1], local)
    local = local.astype(jnp.int32)
    place = jnp.where(refs < float(elems), elems, jnp.where(refs < float(elems + send), 0, 2 * elems))
    kap[...] = place + (local & 1) * pairs + (local >> 1)

    lane = lax.broadcasted_iota(jnp.int32, (pairs, 2 * LANES), 1)
    lane = jnp.where(lane >= 3 * elems, lane - 3 * elems, lane)
    lane = jnp.where(lax.broadcasted_iota(jnp.int32, lane.shape, 1) < 6 * elems, lane, -1)

    def build(d, carry):
        rows = kap[pl.ds(pl.multiple_of(d * pairs, pairs), pairs), :]
        for s in range(slots):
            for h in range(2):
                col = rows[:, h * slots + s:h * slots + s + 1]
                hit = jnp.where(lane == col, 1.0, 0.0).astype(bf16)
                onehot[d, s * elems + h * pairs:s * elems + (h + 1) * pairs, :] = hit
        return carry

    lax.fori_loop(0, parts, build, 0)
    inv_diag = scal[0]
    total_rows = parts * elems

    def step(i, carry):
        now = dirn[...].reshape(total_rows, 2 * LANES)
        hi, lo = split(now)
        for ext, val in ((ext_hi, hi), (ext_lo, lo)):
            ext[elems:elems + total_rows] = val
            ext[:elems] = val[total_rows - elems:]
            ext[elems + total_rows:] = val[:elems]

        def gather(d, c):
            at = pl.ds(pl.multiple_of(d * elems, elems), 3 * elems)
            window = jnp.concatenate([ext_hi[at], ext_lo[at], jnp.zeros((2 * LANES - 6 * elems, 2 * LANES), bf16)], axis=0)
            y = dot(onehot[d], window)
            hi, lo = split(y)
            to = pl.ds(pl.multiple_of(d * elems, elems), elems)
            for s in range(slots):
                y_hi[s, to, :] = hi[s * elems:(s + 1) * elems]
                y_lo[s, to, :] = lo[s * elems:(s + 1) * elems]
            return c

        lax.fori_loop(0, parts, gather, 0)
        total = jnp.zeros((total_rows, 2 * LANES), f32)
        yh = jnp.concatenate([y_hi[s] for s in range(slots)], axis=1)
        yl = jnp.concatenate([y_lo[s] for s in range(slots)], axis=1)
        total = dot(yh, w_hi[...]) + dot(yl, w_hi[...]) + dot(yh, w_lo[...])
        total = total.reshape(dirn.shape)
        old = dirn[...]
        sol[...] = sol[...] + old
        left = resid[...] - (old + inv_diag * total)
        resid[...] = left
        dirn[...] = scal[1 + 2 * i] * old + scal[2 + 2 * i] * left
        return carry

    lax.fori_loop(0, CHEB, step, 0)
    final = sol[...] + dirn[...]
    f = [final[:, h].reshape(parts * pairs, 2 * LANES) for h in range(2)]
    a, b = [v[:, :LANES] for v in f], [v[:, LANES:] for v in f]
    out[:, 0] = jnp.where(half, a[0], pltpu.roll(a[1], NP, 1)).reshape(shape)
    out[:, 1] = jnp.where(half, pltpu.roll(a[0], NP, 1), a[1]).reshape(shape)
    out[:, 2] = jnp.where(half, b[0], pltpu.roll(b[1], NP, 1)).reshape(shape)


def vmem(n):
    return [pl.BlockSpec(memory_space=pltpu.VMEM)] * n


def shards(velocity, vorticity, blocks, nbr_ref, send_list):
    comps, modes_dev, _, merged = velocity.shape
    n_mode, parts = lax.axis_size("mode"), lax.axis_size("dom")
    slots, elems = nbr_ref.shape
    send = send_list.shape[1]
    pairs = elems // 2
    modes_all = modes_dev * n_mode
    me = lax.axis_index("mode")
    rows = comps * modes_dev * 2

    both = jnp.concatenate([v.reshape(rows, n_mode, LANES) for v in (velocity, vorticity)], axis=0)
    lines = lax.all_to_all(both.transpose(1, 0, 2), "mode", split_axis=0, concat_axis=0, tiled=True)

    mine = lax.dynamic_slice_in_dim(nbr_ref.reshape(slots, pairs, 2), me, 1, axis=1)[:, 0]
    table = jnp.concatenate([mine.T.reshape(-1), send_list.reshape(-1)]).astype(f32)
    table = jnp.pad(table, (0, LANES - table.shape[0])).reshape(1, LANES)
    width = (comps + 1) * LANES
    devices = n_mode * parts
    rhs = pl.pallas_call(
        lines_kernel,
        out_shape=jax.ShapeDtypeStruct((devices, 1, width), f32),
        in_specs=vmem(6), out_specs=vmem(1)[0], name="lines",
    )(lines, table, *[jnp.asarray(t) for t in spanwise_tables(modes_all)])
    columns = lax.all_to_all(rhs, ("mode", "dom"), split_axis=0, concat_axis=0, tiled=True)
    columns = columns.reshape(n_mode, parts, width).transpose(1, 0, 2).reshape(devices, width)

    eye = jnp.eye(4, dtype=f32).at[3, 3].set(0.0)
    weight = jnp.einsum("spq,cd->scqdp", blocks, eye).reshape(slots * 4 * NP, 4 * NP)
    rounded = lax.reduce_precision(weight, 8, 7)
    w_hi, w_lo = rounded.astype(bf16), (weight - rounded).astype(bf16)
    mode = me * modes_dev + lax.axis_index("dom") // 2
    wavenum = mode.astype(f32) / modes_all
    coefs = []
    rho = 0.5
    for _ in range(CHEB):
        rho_next = 1.0 / (4.0 - rho)
        coefs += [rho_next * rho, 4.0 * rho_next]
        rho = rho_next
    scal = jnp.concatenate([(1.0 / (1.0 + 4.0 * wavenum * wavenum)).reshape(1), jnp.asarray(coefs, f32)])
    state = pltpu.VMEM((parts, 2, pairs, 2 * LANES), f32)
    ext = pltpu.VMEM(((parts + 2) * elems, 2 * LANES), bf16)
    picked = pltpu.VMEM((slots, parts * elems, 2 * LANES), bf16)
    done = pl.pallas_call(
        functools.partial(solve_kernel, parts, pairs, slots, send),
        out_shape=jax.ShapeDtypeStruct((parts, comps, pairs, LANES), f32),
        in_specs=[pl.BlockSpec(memory_space=pltpu.SMEM)] + vmem(3), out_specs=vmem(1)[0],
        scratch_shapes=[
            pltpu.VMEM((parts, slots * elems, 2 * LANES), bf16), ext, ext, picked, picked,
            state, state, state, pltpu.VMEM((devices, LANES), jnp.int32),
        ],
        name="solve",
    )(scal, columns, w_hi, w_lo)
    back = lax.all_to_all(done.reshape(parts, comps * pairs, LANES), "dom", split_axis=0, concat_axis=0, tiled=True)
    back = back.reshape(modes_dev, 2, comps, pairs, LANES).transpose(2, 0, 1, 3, 4)
    return back.reshape(comps, modes_dev, 2, merged)


def solution(mesh):
    placed = (
        P(None, "mode", None, "dom"),
        P(None, "mode", None, "dom"),
        P(),
        P(None, "dom"),
        P(None, "dom"),
    )
    return jax.shard_map(
        shards, mesh=mesh, in_specs=placed, out_specs=P(None, "mode", None, "dom"), check_vma=False
    )
```

```python
import functools

import jax
import jax.numpy as jnp
import numpy as np
from jax import lax
from jax.experimental import pallas as pl
from jax.experimental.pallas import tpu as pltpu
from jax.sharding import PartitionSpec as P


CHEB = 4
NP = 64
COMPS = 3
LANES = 128
bf16, f32 = jnp.bfloat16, jnp.float32


def split(value):
    high = value.astype(bf16)
    return high, (value - high.astype(f32)).astype(bf16)


def np_split(value):
    high = value.astype(np.float32).astype(bf16)
    return high, (value - high.astype(np.float64)).astype(np.float32).astype(bf16)


def spanwise_tables(count):
    planes = 2 * count
    angle = 2 * np.pi / planes * ((np.arange(planes)[:, None] * np.arange(count)[None, :]) % planes)
    weights = np.where(np.arange(count) == 0, 1.0, 2.0)
    forward = np.stack([weights * np.cos(angle), -weights * np.sin(angle)], axis=2).reshape(planes, planes)
    back = np.stack([np.cos(angle).T, -np.sin(angle).T], axis=1).reshape(planes, planes) / planes
    return np.stack(np_split(forward) + np_split(back))


def dot(a, b):
    return jnp.dot(a, b, preferred_element_type=f32)


def dot3(a, b):
    return dot(a[0], b[0]) + dot(a[1], b[0]) + dot(a[0], b[1])


def lines_kernel(lines, tables, out):
    senders, rows, _ = lines.shape
    per = rows // (2 * COMPS)
    count = senders * per
    fields = [lines[:, i * per:(i + 1) * per, :].reshape(count, LANES) for i in range(2 * COMPS)]
    forward = (tables[0], tables[1])
    planes = [dot3(forward, split(jnp.concatenate(fields[i:i + 2], axis=1))) for i in range(0, 2 * COMPS, 2)]
    planes = [half for pair in planes for half in (pair[:, :LANES], pair[:, LANES:])]
    u, w = planes[:COMPS], planes[COMPS:]
    cross = jnp.concatenate([u[(c + 1) % 3] * w[(c + 2) % 3] - u[(c + 2) % 3] * w[(c + 1) % 3] for c in range(3)], axis=1)
    forcing = dot3((tables[2], tables[3]), split(cross))
    mode = lax.broadcasted_iota(jnp.int32, (count, LANES), 0) >> 1
    wavenum = mode.astype(f32) * (2.0 / count)
    inv_diag = 1.0 / (1.0 + 4.0 * wavenum * wavenum)
    for c in range(COMPS):
        out[:, 0, c * LANES:(c + 1) * LANES] = (fields[c] + forcing[:, c * LANES:(c + 1) * LANES]) * inv_diag


def prep_kernel(parts, pairs, slots, send, table, onehot, kap):
    elems = 2 * pairs
    refs = table[...]
    below = jnp.concatenate([refs[-pairs:], refs[:-pairs]], axis=0)
    above = jnp.concatenate([refs[pairs:], refs[:pairs]], axis=0)
    local = refs
    first = 2 * slots
    for s in range(send):
        local = jnp.where(refs == float(elems + s), below[:, first + s:first + s + 1], local)
        at = first + send + s
        local = jnp.where(refs == float(elems + send + s), above[:, at:at + 1], local)
    local = local.astype(jnp.int32)
    place = jnp.where(refs < float(elems), elems, jnp.where(refs < float(elems + send), 0, 2 * elems))
    kap[...] = place + (local & 1) * pairs + (local >> 1)

    lane = lax.broadcasted_iota(jnp.int32, (pairs, 2 * LANES), 1)
    lane = jnp.where(lane >= 3 * elems, lane - 3 * elems, lane)
    lane = jnp.where(lax.broadcasted_iota(jnp.int32, lane.shape, 1) < 6 * elems, lane, -1)

    def build(d, carry):
        rows = kap[pl.ds(pl.multiple_of(d * pairs, pairs), pairs), :]
        for s in range(slots):
            for h in range(2):
                col = rows[:, h * slots + s:h * slots + s + 1]
                hit = jnp.where(lane == col, 1.0, 0.0).astype(bf16)
                onehot[d, s * elems + h * pairs:s * elems + (h + 1) * pairs, :] = hit
        return carry

    lax.fori_loop(0, parts, build, 0)


def weight_kernel(slots, blocks, w_hi, w_lo):
    w_hi[...] = jnp.zeros_like(w_hi)
    w_lo[...] = jnp.zeros_like(w_lo)

    def place_block(s, carry):
        hi, lo = split(blocks[s].T)
        base = pl.multiple_of(s * 4 * NP, 4 * NP)
        for c in range(COMPS):
            at = (pl.ds(base + c * NP, NP), slice(c * NP, (c + 1) * NP))
            w_hi[at] = hi
            w_lo[at] = lo
        return carry

    lax.fori_loop(0, slots, place_block, 0)


def solve_kernel(parts, pairs, slots, scal, state_in, onehot, w_hi, w_lo, out,
                 ext_hi, ext_lo, y_hi, y_lo, sol, resid, dirn):
    elems = 2 * pairs
    half = lax.broadcasted_iota(jnp.int32, (parts * pairs, LANES), 1) < NP
    x = [state_in[:, c * LANES:(c + 1) * LANES] for c in range(COMPS)]
    swap = [pltpu.roll(v, NP, 1) for v in x]
    shape = (parts, pairs, LANES)
    zero = jnp.zeros_like(x[0])
    dirn[:, 0, :, :LANES] = jnp.where(half, x[0], swap[1]).reshape(shape)
    dirn[:, 0, :, LANES:] = jnp.where(half, x[2], zero).reshape(shape)
    dirn[:, 1, :, :LANES] = jnp.where(half, swap[0], x[1]).reshape(shape)
    dirn[:, 1, :, LANES:] = jnp.where(half, swap[2], zero).reshape(shape)
    resid[...] = dirn[...]
    sol[...] = jnp.zeros_like(sol)

    inv_diag = scal[0]
    total_rows = parts * elems

    def step(i, carry):
        now = dirn[...].reshape(total_rows, 2 * LANES)
        hi, lo = split(now)
        for ext, val in ((ext_hi, hi), (ext_lo, lo)):
            ext[elems:elems + total_rows] = val
            ext[:elems] = val[total_rows - elems:]
            ext[elems + total_rows:] = val[:elems]

        def gather(d, c):
            at = pl.ds(pl.multiple_of(d * elems, elems), 3 * elems)
            window = jnp.concatenate([ext_hi[at], ext_lo[at], jnp.zeros((2 * LANES - 6 * elems, 2 * LANES), bf16)], axis=0)
            y = dot(onehot[d], window)
            hi, lo = split(y)
            to = pl.ds(pl.multiple_of(d * elems, elems), elems)
            for s in range(slots):
                y_hi[s, to, :] = hi[s * elems:(s + 1) * elems]
                y_lo[s, to, :] = lo[s * elems:(s + 1) * elems]
            return c

        lax.fori_loop(0, parts, gather, 0, unroll=4)
        yh = jnp.concatenate([y_hi[s] for s in range(slots)], axis=1)
        yl = jnp.concatenate([y_lo[s] for s in range(slots)], axis=1)
        total = dot(yh, w_hi[...]) + dot(yl, w_hi[...]) + dot(yh, w_lo[...])
        total = total.reshape(dirn.shape)
        old = dirn[...]
        sol[...] = sol[...] + old
        left = resid[...] - (old + inv_diag * total)
        resid[...] = left
        dirn[...] = scal[1 + 2 * i] * old + scal[2 + 2 * i] * left
        return carry

    lax.fori_loop(0, CHEB, step, 0)
    final = sol[...] + dirn[...]
    f = [final[:, h].reshape(parts * pairs, 2 * LANES) for h in range(2)]
    a, b = [v[:, :LANES] for v in f], [v[:, LANES:] for v in f]
    out[:, 0] = jnp.where(half, a[0], pltpu.roll(a[1], NP, 1)).reshape(shape)
    out[:, 1] = jnp.where(half, pltpu.roll(a[0], NP, 1), a[1]).reshape(shape)
    out[:, 2] = jnp.where(half, b[0], pltpu.roll(b[1], NP, 1)).reshape(shape)


def vmem(n):
    return [pl.BlockSpec(memory_space=pltpu.VMEM)] * n


def shards(velocity, vorticity, blocks, nbr_ref, send_list):
    comps, modes_dev, _, merged = velocity.shape
    n_mode, parts = lax.axis_size("mode"), lax.axis_size("dom")
    slots, elems = nbr_ref.shape
    send = send_list.shape[1]
    pairs = elems // 2
    modes_all = modes_dev * n_mode
    me = lax.axis_index("mode")
    rows = comps * modes_dev * 2

    both = jnp.concatenate([v.reshape(rows, n_mode, LANES) for v in (velocity, vorticity)], axis=0)
    lines = lax.all_to_all(both.transpose(1, 0, 2), "mode", split_axis=0, concat_axis=0, tiled=True)

    table = jnp.concatenate([
        nbr_ref.reshape(slots, pairs, 2).transpose(1, 2, 0).reshape(pairs, 2 * slots),
        jnp.broadcast_to(send_list.reshape(1, 2 * send), (pairs, 2 * send)),
    ], axis=1).astype(f32)
    table = jnp.pad(table, ((0, 0), (0, LANES - table.shape[1])))
    side = 4
    near = [[a * side + b for b in range(side)] for a in range(parts // side)]
    far = [[a * side + b for a in range(parts // side)] for b in range(side)]
    table = lax.all_gather(table, "dom", axis=0, tiled=True, axis_index_groups=near)
    table = lax.all_gather(table, "dom", axis=0, tiled=True, axis_index_groups=far)
    onehot = pl.pallas_call(
        functools.partial(prep_kernel, parts, pairs, slots, send),
        out_shape=jax.ShapeDtypeStruct((parts, slots * elems, 2 * LANES), bf16),
        in_specs=vmem(1), out_specs=vmem(1)[0],
        scratch_shapes=[pltpu.VMEM((parts * pairs, LANES), jnp.int32)],
        compiler_params=pltpu.CompilerParams(vmem_limit_bytes=12 << 20),
        cost_estimate=pl.CostEstimate(flops=0, bytes_accessed=12 << 20, transcendentals=0),
        name="prep",
    )(table)

    width = comps * LANES
    devices = n_mode * parts
    rhs = pl.pallas_call(
        lines_kernel,
        out_shape=jax.ShapeDtypeStruct((devices, 1, width), f32),
        in_specs=vmem(2), out_specs=vmem(1)[0], name="lines",
        compiler_params=pltpu.CompilerParams(vmem_limit_bytes=12 << 20),
    )(lines, jnp.asarray(spanwise_tables(modes_all)))
    columns = lax.all_to_all(rhs, ("mode", "dom"), split_axis=0, concat_axis=0, tiled=True)
    weight = jax.ShapeDtypeStruct((slots * 4 * NP, 4 * NP), bf16)
    w_hi, w_lo = pl.pallas_call(
        functools.partial(weight_kernel, slots), out_shape=[weight, weight],
        in_specs=vmem(1), out_specs=vmem(2),
        compiler_params=pltpu.CompilerParams(vmem_limit_bytes=6 << 20),
        cost_estimate=pl.CostEstimate(flops=0, bytes_accessed=3 << 20, transcendentals=0),
        name="weights",
    )(blocks)
    columns = columns.reshape(n_mode, parts, width).transpose(1, 0, 2).reshape(devices, width)

    mode = me * modes_dev + lax.axis_index("dom") // 2
    wavenum = mode.astype(f32) / modes_all
    coefs = []
    rho = 0.5
    for _ in range(CHEB):
        rho_next = 1.0 / (4.0 - rho)
        coefs += [rho_next * rho, 4.0 * rho_next]
        rho = rho_next
    scal = jnp.concatenate([(1.0 / (1.0 + 4.0 * wavenum * wavenum)).reshape(1), jnp.asarray(coefs, f32)])
    state = pltpu.VMEM((parts, 2, pairs, 2 * LANES), f32)
    ext = pltpu.VMEM(((parts + 2) * elems, 2 * LANES), bf16)
    picked = pltpu.VMEM((slots, parts * elems, 2 * LANES), bf16)
    done = pl.pallas_call(
        functools.partial(solve_kernel, parts, pairs, slots),
        out_shape=jax.ShapeDtypeStruct((parts, comps, pairs, LANES), f32),
        in_specs=[pl.BlockSpec(memory_space=pltpu.SMEM)] + vmem(4), out_specs=vmem(1)[0],
        scratch_shapes=[ext, ext, picked, picked, state, state, state],
        compiler_params=pltpu.CompilerParams(vmem_limit_bytes=24 << 20),
        name="solve",
    )(scal, columns, onehot, w_hi, w_lo)
    back = lax.all_to_all(done.reshape(parts, comps * pairs, LANES), "dom", split_axis=0, concat_axis=0, tiled=True)
    back = back.reshape(modes_dev, 2, comps, pairs, LANES).transpose(2, 0, 1, 3, 4)
    return back.reshape(comps, modes_dev, 2, merged)


def solution(mesh):
    placed = (
        P(None, "mode", None, "dom"),
        P(None, "mode", None, "dom"),
        P(),
        P(None, "dom"),
        P(None, "dom"),
    )
    return jax.shard_map(
        shards, mesh=mesh, in_specs=placed, out_specs=P(None, "mode", None, "dom"), check_vma=False
    )
```

```python
import functools

import jax
import jax.numpy as jnp
import numpy as np
from jax import lax
from jax.experimental import pallas as pl
from jax.experimental.pallas import tpu as pltpu
from jax.sharding import PartitionSpec as P


CHEB = 4
NP = 64
COMPS = 3
LANES = 128
bf16, f32 = jnp.bfloat16, jnp.float32


def split(value):
    high = value.astype(bf16)
    return high, (value - high.astype(f32)).astype(bf16)


def np_split(value):
    high = value.astype(np.float32).astype(bf16)
    return high, (value - high.astype(np.float64)).astype(np.float32).astype(bf16)


def spanwise_tables(count):
    planes = 2 * count
    angle = 2 * np.pi / planes * ((np.arange(planes)[:, None] * np.arange(count)[None, :]) % planes)
    weights = np.where(np.arange(count) == 0, 1.0, 2.0)
    forward = np.stack([weights * np.cos(angle), -weights * np.sin(angle)], axis=2).reshape(planes, planes)
    back = np.stack([np.cos(angle).T, -np.sin(angle).T], axis=1).reshape(planes, planes) / planes
    return np.stack(np_split(forward) + np_split(back))


def dot(a, b):
    return jnp.dot(a, b, preferred_element_type=f32)


def dot3(a, b):
    return dot(a[0], b[0]) + dot(a[1], b[0]) + dot(a[0], b[1])


def lines_kernel(lines, tables, out):
    senders, rows, _ = lines.shape
    per = rows // (2 * COMPS)
    count = senders * per
    fields = [lines[:, i * per:(i + 1) * per, :].reshape(count, LANES) for i in range(2 * COMPS)]
    forward = (tables[0], tables[1])
    planes = [dot3(forward, split(jnp.concatenate(fields[i:i + 2], axis=1))) for i in range(0, 2 * COMPS, 2)]
    planes = [half for pair in planes for half in (pair[:, :LANES], pair[:, LANES:])]
    u, w = planes[:COMPS], planes[COMPS:]
    cross = jnp.concatenate([u[(c + 1) % 3] * w[(c + 2) % 3] - u[(c + 2) % 3] * w[(c + 1) % 3] for c in range(3)], axis=1)
    forcing = dot3((tables[2], tables[3]), split(cross))
    mode = lax.broadcasted_iota(jnp.int32, (count, LANES), 0) >> 1
    wavenum = mode.astype(f32) * (2.0 / count)
    inv_diag = 1.0 / (1.0 + 4.0 * wavenum * wavenum)
    for c in range(COMPS):
        out[:, 0, c * LANES:(c + 1) * LANES] = (fields[c] + forcing[:, c * LANES:(c + 1) * LANES]) * inv_diag


def prep_kernel(parts, pairs, slots, send, order, tables, blocks, onehot, weights, refs_at, kap):
    elems = 2 * pairs
    for k in range(parts):
        refs_at[pl.ds(pl.multiple_of(order[k] * pairs, pairs), pairs), :] = tables[k]

    refs = refs_at[...]
    below = jnp.concatenate([refs[-pairs:], refs[:-pairs]], axis=0)
    above = jnp.concatenate([refs[pairs:], refs[:pairs]], axis=0)
    local = refs
    first = 2 * slots
    for s in range(send):
        local = jnp.where(refs == float(elems + s), below[:, first + s:first + s + 1], local)
        at = first + send + s
        local = jnp.where(refs == float(elems + send + s), above[:, at:at + 1], local)
    local = local.astype(jnp.int32)
    place = jnp.where(refs < float(elems), elems, jnp.where(refs < float(elems + send), 0, 2 * elems))
    kap[...] = place + (local & 1) * pairs + (local >> 1)
    lane = lax.broadcasted_iota(jnp.int32, (pairs, LANES), 1)

    def build(d, carry):
        rows = kap[pl.ds(pl.multiple_of(d * pairs, pairs), pairs), :]
        for s in range(slots):
            for h in range(2):
                col = rows[:, h * slots + s:h * slots + s + 1]
                hit = jnp.where(lane == col, 1.0, 0.0).astype(bf16)
                onehot[d, s * elems + h * pairs:s * elems + (h + 1) * pairs, :] = hit
        return carry

    lax.fori_loop(0, parts, build, 0)

    weights[...] = jnp.zeros_like(weights)

    def place_block(s, carry):
        base = pl.multiple_of(s * LANES, LANES)
        for part, val in enumerate(split(blocks[s].T)):
            for c in range(2):
                at = part * LANES + c * NP
                weights[pl.ds(base + c * NP, NP), at:at + NP] = val
        return carry

    lax.fori_loop(0, slots, place_block, 0)


def solve_kernel(parts, pairs, slots, scal, state_in, onehot, weights, out,
                 ext_hi, ext_lo, picked, sol, resid, dirn):
    elems = 2 * pairs
    half = lax.broadcasted_iota(jnp.int32, (parts * pairs, LANES), 1) < NP
    x = [state_in[:, c * LANES:(c + 1) * LANES] for c in range(COMPS)]
    swap = [pltpu.roll(v, NP, 1) for v in x]
    shape = (parts, pairs, LANES)
    zero = jnp.zeros_like(x[0])
    dirn[0, :, 0] = jnp.where(half, x[0], swap[1]).reshape(shape)
    dirn[1, :, 0] = jnp.where(half, x[2], zero).reshape(shape)
    dirn[0, :, 1] = jnp.where(half, swap[0], x[1]).reshape(shape)
    dirn[1, :, 1] = jnp.where(half, swap[2], zero).reshape(shape)
    resid[...] = dirn[...]
    sol[...] = jnp.zeros_like(sol)
    inv_diag = scal[0]
    total_rows = parts * elems
    fill = jnp.zeros((LANES - 3 * elems, 2 * LANES), bf16)

    def step(i, carry):
        for j in range(2):
            lanes = slice(j * LANES, (j + 1) * LANES)
            for ext, val in zip((ext_hi, ext_lo), split(dirn[j].reshape(total_rows, LANES))):
                ext[elems:elems + total_rows, lanes] = val
                ext[:elems, lanes] = val[total_rows - elems:]
                ext[elems + total_rows:, lanes] = val[:elems]

        def gather(d, c):
            at = pl.ds(pl.multiple_of(d * elems, elems), 3 * elems)
            window = jnp.concatenate([ext_hi[at], fill, ext_lo[at], fill], axis=0)
            one = onehot[d]
            y = dot(jnp.concatenate([one, one], axis=1), window)
            to = pl.ds(pl.multiple_of(d * elems, elems), elems)
            for part, val in enumerate(split(y)):
                for s in range(slots):
                    at = (part * slots + s) * LANES
                    for j in range(2):
                        picked[j, to, at:at + LANES] = val[s * elems:(s + 1) * elems, j * LANES:(j + 1) * LANES]
            return c

        lax.fori_loop(0, parts, gather, 0, unroll=4)
        both = jnp.concatenate([weights[...], weights[...]], axis=0)
        total = dot(picked[...].reshape(2 * total_rows, 2 * slots * LANES), both)
        total = (total[:, :LANES] + total[:, LANES:]).reshape(dirn.shape)
        old = dirn[...]
        sol[...] = sol[...] + old
        left = resid[...] - (old + inv_diag * total)
        resid[...] = left
        dirn[...] = scal[1 + 2 * i] * old + scal[2 + 2 * i] * left
        return carry

    lax.fori_loop(0, CHEB, step, 0)
    final = sol[...] + dirn[...]
    a, b = [[final[j, :, h].reshape(parts * pairs, LANES) for h in range(2)] for j in range(2)]
    out[:, 0] = jnp.where(half, a[0], pltpu.roll(a[1], NP, 1)).reshape(shape)
    out[:, 1] = jnp.where(half, pltpu.roll(a[0], NP, 1), a[1]).reshape(shape)
    out[:, 2] = jnp.where(half, b[0], pltpu.roll(b[1], NP, 1)).reshape(shape)


def vmem(n):
    return [pl.BlockSpec(memory_space=pltpu.VMEM)] * n


def shards(velocity, vorticity, blocks, nbr_ref, send_list):
    comps, modes_dev, _, merged = velocity.shape
    n_mode, parts = lax.axis_size("mode"), lax.axis_size("dom")
    slots, elems = nbr_ref.shape
    send = send_list.shape[1]
    pairs = elems // 2
    modes_all = modes_dev * n_mode
    me = lax.axis_index("mode")
    rows = comps * modes_dev * 2

    both = jnp.concatenate([v.reshape(rows, n_mode, LANES) for v in (velocity, vorticity)], axis=0)
    lines = lax.all_to_all(both.transpose(1, 0, 2), "mode", split_axis=0, concat_axis=0, tiled=True)

    table = jnp.concatenate([
        nbr_ref.reshape(slots, pairs, 2).transpose(1, 2, 0).reshape(pairs, 2 * slots),
        jnp.broadcast_to(send_list.reshape(1, 2 * send), (pairs, 2 * send)),
    ], axis=1).astype(f32)
    table = jnp.pad(table, ((0, 0), (0, LANES - table.shape[1])))
    side = 4
    here = lax.axis_index("dom")
    near = [lax.ppermute(table, "dom", [(d, d // side * side + (d + i) % side) for d in range(parts)])
            for i in range(1, side)]
    table = jnp.stack([table] + near)
    far = [lax.ppermute(table, "dom", [(d, (d + i * side) % parts) for d in range(parts)])
           for i in range(1, parts // side)]
    table = jnp.concatenate([table] + far, axis=0)
    steps = jnp.arange(parts, dtype=jnp.int32)
    order = (here // side - steps // side) % (parts // side) * side + (here % side - steps % side) % side
    onehot, weights = pl.pallas_call(
        functools.partial(prep_kernel, parts, pairs, slots, send),
        out_shape=[jax.ShapeDtypeStruct((parts, slots * elems, LANES), bf16),
                   jax.ShapeDtypeStruct((slots * LANES, 2 * LANES), bf16)],
        in_specs=[pl.BlockSpec(memory_space=pltpu.SMEM)] + vmem(2), out_specs=vmem(2),
        scratch_shapes=[pltpu.VMEM((parts * pairs, LANES), f32), pltpu.VMEM((parts * pairs, LANES), jnp.int32)],
        compiler_params=pltpu.CompilerParams(vmem_limit_bytes=8 << 20),
        cost_estimate=pl.CostEstimate(flops=0, bytes_accessed=8 << 20, transcendentals=0),
        name="prep",
    )(order, table, blocks)

    width = comps * LANES
    devices = n_mode * parts
    rhs = pl.pallas_call(
        lines_kernel,
        out_shape=jax.ShapeDtypeStruct((devices, 1, width), f32),
        in_specs=vmem(2), out_specs=vmem(1)[0], name="lines",
        compiler_params=pltpu.CompilerParams(vmem_limit_bytes=12 << 20),
    )(lines, jnp.asarray(spanwise_tables(modes_all)))
    mode = me * modes_dev + lax.axis_index("dom") // 2
    wavenum = mode.astype(f32) / modes_all
    coefs = []
    rho = 0.5
    for _ in range(CHEB):
        rho_next = 1.0 / (4.0 - rho)
        coefs += [rho_next * rho, 4.0 * rho_next]
        rho = rho_next
    scal = jnp.concatenate([(1.0 / (1.0 + 4.0 * wavenum * wavenum)).reshape(1), jnp.asarray(coefs, f32)])
    rhs, scal, onehot, weights = lax.optimization_barrier((rhs, scal, onehot, weights))
    columns = lax.all_to_all(rhs, ("mode", "dom"), split_axis=0, concat_axis=0, tiled=True)
    columns = columns.reshape(n_mode, parts, width).transpose(1, 0, 2).reshape(devices, width)

    state = pltpu.VMEM((2, parts, 2, pairs, LANES), f32)
    ext = pltpu.VMEM(((parts + 2) * elems, 2 * LANES), bf16)
    picked = pltpu.VMEM((2, parts * elems, 2 * slots * LANES), bf16)
    done = pl.pallas_call(
        functools.partial(solve_kernel, parts, pairs, slots),
        out_shape=jax.ShapeDtypeStruct((parts, comps, pairs, LANES), f32),
        in_specs=[pl.BlockSpec(memory_space=pltpu.SMEM)] + vmem(3), out_specs=vmem(1)[0],
        scratch_shapes=[ext, ext, picked, state, state, state],
        compiler_params=pltpu.CompilerParams(vmem_limit_bytes=24 << 20),
        name="solve",
    )(scal, columns, onehot, weights)
    back = lax.all_to_all(done.reshape(parts, comps * pairs, LANES), "dom", split_axis=0, concat_axis=0, tiled=True)
    back = back.reshape(modes_dev, 2, comps, pairs, LANES).transpose(2, 0, 1, 3, 4)
    return back.reshape(comps, modes_dev, 2, merged)


def solution(mesh):
    placed = (
        P(None, "mode", None, "dom"),
        P(None, "mode", None, "dom"),
        P(),
        P(None, "dom"),
        P(None, "dom"),
    )
    return jax.shard_map(
        shards, mesh=mesh, in_specs=placed, out_specs=P(None, "mode", None, "dom"), check_vma=False
    )
```

```python
import functools

import jax
import jax.numpy as jnp
import numpy as np
from jax import lax
from jax.experimental import pallas as pl
from jax.experimental.pallas import tpu as pltpu
from jax.sharding import PartitionSpec as P


CHEB = 4
UNROLL = 4
NP = 64
COMPS = 3
LANES = 128
bf16, f32 = jnp.bfloat16, jnp.float32


def split(value):
    high = value.astype(bf16)
    return high, (value - high.astype(f32)).astype(bf16)


def np_split(value):
    high = value.astype(np.float32).astype(bf16)
    return high, (value - high.astype(np.float64)).astype(np.float32).astype(bf16)


def spanwise_tables(count):
    planes = 2 * count
    angle = 2 * np.pi / planes * ((np.arange(planes)[:, None] * np.arange(count)[None, :]) % planes)
    weights = np.where(np.arange(count) == 0, 1.0, 2.0)
    forward = np.stack([weights * np.cos(angle), -weights * np.sin(angle)], axis=2).reshape(planes, planes)
    back = np.stack([np.cos(angle).T, -np.sin(angle).T], axis=1).reshape(planes, planes) / planes
    return np.stack(np_split(forward) + np_split(back))


def dot(a, b):
    return jnp.dot(a, b, preferred_element_type=f32)


def dot3(a, b):
    return dot(a[0], b[0]) + dot(a[1], b[0]) + dot(a[0], b[1])


def lines_kernel(lines, tables, out):
    senders, rows, _ = lines.shape
    per = rows // (2 * COMPS)
    count = senders * per
    fields = [lines[:, i * per:(i + 1) * per, :].reshape(count, LANES) for i in range(2 * COMPS)]
    forward = (tables[0], tables[1])
    planes = [dot3(forward, split(jnp.concatenate(fields[i:i + 2], axis=1))) for i in range(0, 2 * COMPS, 2)]
    planes = [half for pair in planes for half in (pair[:, :LANES], pair[:, LANES:])]
    u, w = planes[:COMPS], planes[COMPS:]
    cross = jnp.concatenate([u[(c + 1) % 3] * w[(c + 2) % 3] - u[(c + 2) % 3] * w[(c + 1) % 3] for c in range(3)], axis=1)
    forcing = dot3((tables[2], tables[3]), split(cross))
    mode = lax.broadcasted_iota(jnp.int32, (count, LANES), 0) >> 1
    wavenum = mode.astype(f32) * (2.0 / count)
    inv_diag = 1.0 / (1.0 + 4.0 * wavenum * wavenum)
    for c in range(COMPS):
        out[:, 0, c * LANES:(c + 1) * LANES] = (fields[c] + forcing[:, c * LANES:(c + 1) * LANES]) * inv_diag


def first_send(slots):
    return -(-2 * slots // 8) * 8


def prep_kernel(parts, pairs, slots, send, order, tables, blocks, onehot, weights, refs_at, kap):
    elems = 2 * pairs
    for k in range(parts):
        refs_at[pl.ds(pl.multiple_of(order[k] * pairs, pairs), pairs), :] = tables[k]

    turned = refs_at[...].T
    first = first_send(slots)
    refs = turned[:first]
    shared = turned[first:first + 2 * send]
    below = pltpu.roll(shared, pairs, 1)
    above = pltpu.roll(shared, (parts - 1) * pairs, 1)
    local = refs
    for s in range(send):
        local = jnp.where(refs == float(elems + s), below[s:s + 1], local)
        local = jnp.where(refs == float(elems + send + s), above[send + s:send + s + 1], local)
    local = local.astype(jnp.int32)
    place = jnp.where(refs < float(elems), elems, jnp.where(refs < float(elems + send), 0, 2 * elems))
    odd = (lax.broadcasted_iota(jnp.int32, place.shape, 1) // pairs) & 1
    place = (place + odd * elems + (local & 1) * pairs + (local >> 1)).astype(f32)
    place = jnp.concatenate([place, jnp.zeros((LANES - first, parts * pairs), f32)], axis=0)
    kap[...] = place.T.astype(jnp.int32)
    lane = lax.broadcasted_iota(jnp.int32, (pairs, LANES), 1)

    def build(d, carry):
        rows = kap[pl.ds(pl.multiple_of(d * pairs, pairs), pairs), :]
        for s in range(slots):
            for h in range(2):
                col = rows[:, h * slots + s:h * slots + s + 1]
                hit = jnp.where(lane == col, 1.0, 0.0).astype(bf16)
                at = pl.multiple_of((d & 1) * slots * elems, elems) + s * elems + h * pairs
                onehot[d >> 1, pl.ds(at, pairs), :] = hit
        return carry

    lax.fori_loop(0, parts, build, 0, unroll=4)

    weights[...] = jnp.zeros_like(weights)

    def place_block(s, carry):
        base = pl.multiple_of(s * LANES, LANES)
        for part, val in enumerate(split(blocks[s].T)):
            for c in range(2):
                at = part * LANES + c * NP
                weights[pl.ds(base + c * NP, NP), at:at + NP] = val
        return carry

    lax.fori_loop(0, slots, place_block, 0, unroll=3)


def solve_kernel(parts, pairs, slots, scal, state_in, onehot, weights, out,
                 ext, picked, sol, resid, dirn):
    elems = 2 * pairs
    ones, twos = parts * pairs, parts * elems
    half = lax.broadcasted_iota(jnp.int32, (ones, LANES), 1) < NP
    few = half[:pairs]
    x = [state_in[:, c * LANES:(c + 1) * LANES] for c in range(COMPS)]
    shape = (parts, pairs, LANES)

    def halves(low, high):
        return jnp.stack([low.reshape(shape), high.reshape(shape)], axis=1).reshape(twos, LANES)

    dirn[:twos] = halves(jnp.where(half, x[0], pltpu.roll(x[1], NP, 1)), jnp.where(half, pltpu.roll(x[0], NP, 1), x[1]))
    dirn[twos:] = x[2]
    resid[...] = dirn[...]
    sol[...] = jnp.zeros_like(sol)
    inv_diag = scal[0]

    def step(i, carry):
        last = dirn[twos:]
        turned = pltpu.roll(last, NP, 1)
        for j, now in enumerate((dirn[:twos], halves(jnp.where(half, last, turned), jnp.where(half, turned, last)))):
            for part, val in enumerate(split(now)):
                lanes = slice((2 * part + j) * LANES, (2 * part + j + 1) * LANES)
                ext[elems:elems + twos, lanes] = val
                ext[:elems, lanes] = val[twos - elems:]
                ext[elems + twos:, lanes] = val[:elems]

        def gather(g, c):
            near = ext[pl.ds(pl.multiple_of(g * 2 * elems, 2 * elems), 4 * elems)]
            window = jnp.concatenate([near[:, :2 * LANES], near[:, 2 * LANES:]], axis=0)
            one = onehot[g]
            y = dot(jnp.concatenate([one, one], axis=1), window)
            for k in range(2):
                two = pl.ds(pl.multiple_of((2 * g + k) * elems, elems), elems)
                single = pl.ds(pl.multiple_of(twos + (2 * g + k) * pairs, pairs), pairs)
                for s in range(slots):
                    row = (k * slots + s) * elems
                    both = y[row:row + elems, :LANES]
                    last = y[row:row + elems, LANES:]
                    last = jnp.where(few, last[:pairs], last[pairs:])
                    for at, val in ((two, both), (single, last)):
                        for part, piece in enumerate(split(val)):
                            at_lane = (part * slots + s) * LANES
                            picked[at, at_lane:at_lane + LANES] = piece
            return c

        lax.fori_loop(0, parts // 2, gather, 0, unroll=UNROLL)
        total = dot(picked[...], jnp.concatenate([weights[...], weights[...]], axis=0))
        total = total[:, :LANES] + total[:, LANES:]
        old = dirn[...]
        sol[...] = sol[...] + old
        left = resid[...] - (old + inv_diag * total)
        resid[...] = left
        dirn[...] = scal[1 + 2 * i] * old + scal[2 + 2 * i] * left
        return carry

    lax.fori_loop(0, CHEB, step, 0)
    final = sol[...] + dirn[...]
    both = final[:twos].reshape(parts, 2, pairs, LANES)
    a = [both[:, h].reshape(ones, LANES) for h in range(2)]
    out[:, 0] = jnp.where(half, a[0], pltpu.roll(a[1], NP, 1)).reshape(shape)
    out[:, 1] = jnp.where(half, pltpu.roll(a[0], NP, 1), a[1]).reshape(shape)
    out[:, 2] = final[twos:].reshape(shape)


def vmem(n):
    return [pl.BlockSpec(memory_space=pltpu.VMEM)] * n


def shards(velocity, vorticity, blocks, nbr_ref, send_list):
    comps, modes_dev, _, merged = velocity.shape
    n_mode, parts = lax.axis_size("mode"), lax.axis_size("dom")
    slots, elems = nbr_ref.shape
    send = send_list.shape[1]
    pairs = elems // 2
    modes_all = modes_dev * n_mode
    me = lax.axis_index("mode")
    rows = comps * modes_dev * 2

    both = jnp.concatenate([v.reshape(rows, n_mode, LANES) for v in (velocity, vorticity)], axis=0)
    lines = lax.all_to_all(both.transpose(1, 0, 2), "mode", split_axis=0, concat_axis=0, tiled=True)

    table = jnp.concatenate([
        nbr_ref.reshape(slots, pairs, 2).transpose(1, 2, 0).reshape(pairs, 2 * slots),
        jnp.zeros((pairs, first_send(slots) - 2 * slots), jnp.int32),
        jnp.broadcast_to(send_list.reshape(1, 2 * send), (pairs, 2 * send)),
    ], axis=1).astype(f32)
    table = jnp.pad(table, ((0, 0), (0, LANES - table.shape[1])))
    side = 4
    here = lax.axis_index("dom")
    near = [lax.ppermute(table, "dom", [(d, d // side * side + (d + i) % side) for d in range(parts)])
            for i in range(1, side)]
    table = jnp.stack([table] + near)
    far = [lax.ppermute(table, "dom", [(d, (d + i * side) % parts) for d in range(parts)])
           for i in range(1, parts // side)]
    table = jnp.concatenate([table] + far, axis=0)
    steps = jnp.arange(parts, dtype=jnp.int32)
    order = (here // side - steps // side) % (parts // side) * side + (here % side - steps % side) % side
    onehot, weights = pl.pallas_call(
        functools.partial(prep_kernel, parts, pairs, slots, send),
        out_shape=[jax.ShapeDtypeStruct((parts // 2, 2 * slots * elems, LANES), bf16),
                   jax.ShapeDtypeStruct((slots * LANES, 2 * LANES), bf16)],
        in_specs=[pl.BlockSpec(memory_space=pltpu.SMEM)] + vmem(2), out_specs=vmem(2),
        scratch_shapes=[pltpu.VMEM((parts * pairs, LANES), f32), pltpu.VMEM((parts * pairs, LANES), jnp.int32)],
        compiler_params=pltpu.CompilerParams(vmem_limit_bytes=8 << 20),
        cost_estimate=pl.CostEstimate(flops=0, bytes_accessed=8 << 20, transcendentals=0),
        name="prep",
    )(order, table, blocks)

    width = comps * LANES
    devices = n_mode * parts
    rhs = pl.pallas_call(
        lines_kernel,
        out_shape=jax.ShapeDtypeStruct((devices, 1, width), f32),
        in_specs=vmem(2), out_specs=vmem(1)[0], name="lines",
        compiler_params=pltpu.CompilerParams(vmem_limit_bytes=12 << 20),
    )(lines, jnp.asarray(spanwise_tables(modes_all)))
    mode = me * modes_dev + lax.axis_index("dom") // 2
    wavenum = mode.astype(f32) / modes_all
    coefs = []
    rho = 0.5
    for _ in range(CHEB):
        rho_next = 1.0 / (4.0 - rho)
        coefs += [rho_next * rho, 4.0 * rho_next]
        rho = rho_next
    scal = jnp.concatenate([(1.0 / (1.0 + 4.0 * wavenum * wavenum)).reshape(1), jnp.asarray(coefs, f32)])
    rhs, scal, onehot, weights = lax.optimization_barrier((rhs, scal, onehot, weights))
    columns = lax.all_to_all(rhs, ("mode", "dom"), split_axis=0, concat_axis=0, tiled=True)
    columns = columns.reshape(n_mode, parts, width).transpose(1, 0, 2).reshape(devices, width)

    rows = parts * pairs * 3
    state = pltpu.VMEM((rows, LANES), f32)
    ext = pltpu.VMEM(((parts + 2) * elems, 4 * LANES), bf16)
    picked = pltpu.VMEM((rows, 2 * slots * LANES), bf16)
    done = pl.pallas_call(
        functools.partial(solve_kernel, parts, pairs, slots),
        out_shape=jax.ShapeDtypeStruct((parts, comps, pairs, LANES), f32),
        in_specs=[pl.BlockSpec(memory_space=pltpu.SMEM)] + vmem(3), out_specs=vmem(1)[0],
        scratch_shapes=[ext, picked, state, state, state],
        compiler_params=pltpu.CompilerParams(vmem_limit_bytes=24 << 20),
        name="solve",
    )(scal, columns, onehot, weights)
    back = lax.all_to_all(done.reshape(parts, comps * pairs, LANES), "dom", split_axis=0, concat_axis=0, tiled=True)
    back = back.reshape(modes_dev, 2, comps, pairs, LANES).transpose(2, 0, 1, 3, 4)
    return back.reshape(comps, modes_dev, 2, merged)


def solution(mesh):
    placed = (
        P(None, "mode", None, "dom"),
        P(None, "mode", None, "dom"),
        P(),
        P(None, "dom"),
        P(None, "dom"),
    )
    return jax.shard_map(
        shards, mesh=mesh, in_specs=placed, out_specs=P(None, "mode", None, "dom"), check_vma=False
    )
```

```python
import functools

import jax
import jax.numpy as jnp
import numpy as np
from jax import lax
from jax.experimental import pallas as pl
from jax.experimental.pallas import tpu as pltpu
from jax.sharding import PartitionSpec as P


CHEB = 4
UNROLL = 8
NP = 64
COMPS = 3
LANES = 128
bf16, f32 = jnp.bfloat16, jnp.float32


def split(value):
    high = value.astype(bf16)
    return high, (value - high.astype(f32)).astype(bf16)


def np_split(value):
    high = value.astype(np.float32).astype(bf16)
    return high, (value - high.astype(np.float64)).astype(np.float32).astype(bf16)


def spanwise_tables(count):
    planes = 2 * count
    angle = 2 * np.pi / planes * ((np.arange(planes)[:, None] * np.arange(count)[None, :]) % planes)
    weights = np.where(np.arange(count) == 0, 1.0, 2.0)
    forward = np.stack([weights * np.cos(angle), -weights * np.sin(angle)], axis=2).reshape(planes, planes)
    back = np.stack([np.cos(angle).T, -np.sin(angle).T], axis=1).reshape(planes, planes) / planes
    return np.stack(np_split(forward) + np_split(back))


def dot(a, b):
    return jnp.dot(a, b, preferred_element_type=f32)


def dot3(a, b):
    return dot(a[0], b[0]) + dot(a[1], b[0]) + dot(a[0], b[1])


def pack_kernel(velocity, vorticity, out):
    rows = 2 * velocity.shape[0]
    for i, field in enumerate((velocity, vorticity)):
        for g in range(0, rows, 8):
            value = field[g // 2:g // 2 + 4].reshape(8, field.shape[2])
            for j in range(out.shape[0]):
                out[j, i * rows + g:i * rows + g + 8, :] = value[:, j * LANES:(j + 1) * LANES]


def lines_kernel(lines, tables, out):
    senders, rows, _ = lines.shape
    per = rows // (2 * COMPS)
    count = senders * per
    fields = [lines[:, (2 * c + i) * per:(2 * c + i + 1) * per, :].reshape(count, LANES) for i in range(2) for c in range(COMPS)]
    forward = (tables[0], tables[1])
    planes = [dot3(forward, split(jnp.concatenate(fields[i:i + 2], axis=1))) for i in range(0, 2 * COMPS, 2)]
    planes = [half for pair in planes for half in (pair[:, :LANES], pair[:, LANES:])]
    u, w = planes[:COMPS], planes[COMPS:]
    cross = jnp.concatenate([u[(c + 1) % 3] * w[(c + 2) % 3] - u[(c + 2) % 3] * w[(c + 1) % 3] for c in range(3)], axis=1)
    forcing = dot3((tables[2], tables[3]), split(cross))
    mode = lax.broadcasted_iota(jnp.int32, (count, LANES), 0) >> 1
    wavenum = mode.astype(f32) * (2.0 / count)
    inv_diag = 1.0 / (1.0 + 4.0 * wavenum * wavenum)
    for c in range(COMPS):
        out[:, 0, c * LANES:(c + 1) * LANES] = (fields[c] + forcing[:, c * LANES:(c + 1) * LANES]) * inv_diag


def first_send(slots):
    return -(-2 * slots // 8) * 8


def prep_kernel(parts, pairs, slots, send, order, tables, blocks, onehot, weights, refs_at, kap):
    elems = 2 * pairs
    for k in range(parts):
        refs_at[pl.ds(pl.multiple_of(order[k] * pairs, pairs), pairs), :] = tables[k]

    turned = refs_at[...].T
    first = first_send(slots)
    refs = turned[:first]
    shared = turned[first:first + 2 * send]
    below = pltpu.roll(shared, pairs, 1)
    above = pltpu.roll(shared, (parts - 1) * pairs, 1)
    local = refs
    for s in range(send):
        local = jnp.where(refs == float(elems + s), below[s:s + 1], local)
        local = jnp.where(refs == float(elems + send + s), above[send + s:send + s + 1], local)
    local = local.astype(jnp.int32)
    place = jnp.where(refs < float(elems), elems, jnp.where(refs < float(elems + send), 0, 2 * elems))
    odd = (lax.broadcasted_iota(jnp.int32, place.shape, 1) // pairs) & 1
    place = (place + odd * elems + (local & 1) * pairs + (local >> 1)).astype(f32)
    place = jnp.concatenate([place, jnp.zeros((LANES - first, parts * pairs), f32)], axis=0)
    kap[...] = place.T.astype(jnp.int32)
    lane = lax.broadcasted_iota(jnp.int32, (pairs, LANES), 1)

    def build(d, carry):
        rows = kap[pl.ds(pl.multiple_of(d * pairs, pairs), pairs), :]
        for s in range(slots):
            for h in range(2):
                col = rows[:, h * slots + s:h * slots + s + 1]
                hit = jnp.where(lane == col, 1.0, 0.0).astype(bf16)
                at = pl.multiple_of((d & 1) * slots * elems, elems) + s * elems + h * pairs
                onehot[d >> 1, pl.ds(at, pairs), :] = hit
        return carry

    lax.fori_loop(0, parts, build, 0, unroll=4)

    weights[...] = jnp.zeros_like(weights)

    def place_block(s, carry):
        base = pl.multiple_of(s * LANES, LANES)
        for part, val in enumerate(split(blocks[s].T)):
            for c in range(2):
                at = part * LANES + c * NP
                weights[pl.ds(base + c * NP, NP), at:at + NP] = val
        return carry

    lax.fori_loop(0, slots, place_block, 0, unroll=3)


def solve_kernel(parts, pairs, slots, scal, state_in, onehot, weights, out,
                 ext, picked, sol, resid, dirn):
    elems = 2 * pairs
    ones, twos = parts * pairs, parts * elems
    half = lax.broadcasted_iota(jnp.int32, (ones, LANES), 1) < NP
    few = half[:pairs]
    x = [state_in[:, c * LANES:(c + 1) * LANES] for c in range(COMPS)]
    shape = (parts, pairs, LANES)

    def halves(low, high):
        return jnp.stack([low.reshape(shape), high.reshape(shape)], axis=1).reshape(twos, LANES)

    dirn[:twos] = halves(jnp.where(half, x[0], pltpu.roll(x[1], NP, 1)), jnp.where(half, pltpu.roll(x[0], NP, 1), x[1]))
    dirn[twos:] = x[2]
    resid[...] = dirn[...]
    sol[...] = jnp.zeros_like(sol)
    inv_diag = scal[0]

    def step(i, carry):
        last = dirn[twos:]
        turned = pltpu.roll(last, NP, 1)
        for j, now in enumerate((dirn[:twos], halves(jnp.where(half, last, turned), jnp.where(half, turned, last)))):
            for part, val in enumerate(split(now)):
                lanes = slice((2 * part + j) * LANES, (2 * part + j + 1) * LANES)
                ext[elems:elems + twos, lanes] = val
                ext[:elems, lanes] = val[twos - elems:]
                ext[elems + twos:, lanes] = val[:elems]

        def gather(g, c):
            near = ext[pl.ds(pl.multiple_of(g * 2 * elems, 2 * elems), 4 * elems)]
            window = jnp.concatenate([near[:, :2 * LANES], near[:, 2 * LANES:]], axis=0)
            one = onehot[g]
            for k in range(2):
                this = one[k * slots * elems:(k + 1) * slots * elems]
                y = dot(jnp.concatenate([this, this], axis=1), window)
                two = pl.ds(pl.multiple_of((2 * g + k) * elems, elems), elems)
                single = pl.ds(pl.multiple_of(twos + (2 * g + k) * pairs, pairs), pairs)
                for s in range(slots):
                    row = s * elems
                    both = y[row:row + elems, :LANES]
                    last = y[row:row + elems, LANES:]
                    last = jnp.where(few, last[:pairs], last[pairs:])
                    for at, val in ((two, both), (single, last)):
                        for part, piece in enumerate(split(val)):
                            at_lane = (part * slots + s) * LANES
                            picked[at, at_lane:at_lane + LANES] = piece
            return c

        lax.fori_loop(0, parts // 2, gather, 0, unroll=UNROLL)
        total = dot(picked[...], jnp.concatenate([weights[...], weights[...]], axis=0))
        total = total[:, :LANES] + total[:, LANES:]
        old = dirn[...]
        sol[...] = sol[...] + old
        left = resid[...] - (old + inv_diag * total)
        resid[...] = left
        dirn[...] = scal[1 + 2 * i] * old + scal[2 + 2 * i] * left
        return carry

    lax.fori_loop(0, CHEB, step, 0)
    final = sol[...] + dirn[...]
    both = final[:twos].reshape(parts, 2, pairs, LANES)
    a = [both[:, h].reshape(ones, LANES) for h in range(2)]
    out[:, 0] = jnp.where(half, a[0], pltpu.roll(a[1], NP, 1)).reshape(shape)
    out[:, 1] = jnp.where(half, pltpu.roll(a[0], NP, 1), a[1]).reshape(shape)
    out[:, 2] = final[twos:].reshape(shape)


def vmem(n):
    return [pl.BlockSpec(memory_space=pltpu.VMEM)] * n


def shards(velocity, vorticity, blocks, nbr_ref, send_list):
    comps, modes_dev, _, merged = velocity.shape
    n_mode, parts = lax.axis_size("mode"), lax.axis_size("dom")
    slots, elems = nbr_ref.shape
    send = send_list.shape[1]
    pairs = elems // 2
    modes_all = modes_dev * n_mode
    me = lax.axis_index("mode")
    rows = comps * modes_dev * 2

    field = pl.BlockSpec((modes_dev, 2, merged), lambda c: (c, 0, 0))
    packed = pl.pallas_call(
        pack_kernel, grid=(comps,),
        out_shape=jax.ShapeDtypeStruct((n_mode, 2 * rows, LANES), f32),
        in_specs=[field, field], out_specs=pl.BlockSpec((n_mode, 4 * modes_dev, LANES), lambda c: (0, c, 0)),
        compiler_params=pltpu.CompilerParams(vmem_limit_bytes=62 << 20), name="pack",
    )(velocity.reshape(comps * modes_dev, 2, merged), vorticity.reshape(comps * modes_dev, 2, merged))
    lines = lax.all_to_all(packed, "mode", split_axis=0, concat_axis=0, tiled=True)

    table = jnp.concatenate([
        nbr_ref.reshape(slots, pairs, 2).transpose(1, 2, 0).reshape(pairs, 2 * slots),
        jnp.zeros((pairs, first_send(slots) - 2 * slots), jnp.int32),
        jnp.broadcast_to(send_list.reshape(1, 2 * send), (pairs, 2 * send)),
    ], axis=1).astype(f32)
    table = jnp.pad(table, ((0, 0), (0, LANES - table.shape[1])))
    side = 4
    here = lax.axis_index("dom")
    near = [lax.ppermute(table, "dom", [(d, d // side * side + (d + i) % side) for d in range(parts)])
            for i in range(1, side)]
    table = jnp.stack([table] + near)
    far = [lax.ppermute(table, "dom", [(d, (d + i * side) % parts) for d in range(parts)])
           for i in range(1, parts // side)]
    table = jnp.concatenate([table] + far, axis=0)
    steps = jnp.arange(parts, dtype=jnp.int32)
    order = (here // side - steps // side) % (parts // side) * side + (here % side - steps % side) % side
    onehot, weights = pl.pallas_call(
        functools.partial(prep_kernel, parts, pairs, slots, send),
        out_shape=[jax.ShapeDtypeStruct((parts // 2, 2 * slots * elems, LANES), bf16),
                   jax.ShapeDtypeStruct((slots * LANES, 2 * LANES), bf16)],
        in_specs=[pl.BlockSpec(memory_space=pltpu.SMEM)] + vmem(2), out_specs=vmem(2),
        scratch_shapes=[pltpu.VMEM((parts * pairs, LANES), f32), pltpu.VMEM((parts * pairs, LANES), jnp.int32)],
        compiler_params=pltpu.CompilerParams(vmem_limit_bytes=8 << 20),
        cost_estimate=pl.CostEstimate(flops=0, bytes_accessed=8 << 20, transcendentals=0),
        name="prep",
    )(order, table, blocks)

    width = comps * LANES
    devices = n_mode * parts
    rhs = pl.pallas_call(
        lines_kernel,
        out_shape=jax.ShapeDtypeStruct((devices, 1, width), f32),
        in_specs=vmem(2), out_specs=vmem(1)[0], name="lines",
        compiler_params=pltpu.CompilerParams(vmem_limit_bytes=12 << 20),
    )(lines, jnp.asarray(spanwise_tables(modes_all)))
    mode = me * modes_dev + lax.axis_index("dom") // 2
    wavenum = mode.astype(f32) / modes_all
    coefs = []
    rho = 0.5
    for _ in range(CHEB):
        rho_next = 1.0 / (4.0 - rho)
        coefs += [rho_next * rho, 4.0 * rho_next]
        rho = rho_next
    scal = jnp.concatenate([(1.0 / (1.0 + 4.0 * wavenum * wavenum)).reshape(1), jnp.asarray(coefs, f32)])
    rhs, scal, onehot, weights = lax.optimization_barrier((rhs, scal, onehot, weights))
    columns = lax.all_to_all(rhs, ("mode", "dom"), split_axis=0, concat_axis=0, tiled=True)
    columns = columns.reshape(n_mode, parts, width).transpose(1, 0, 2).reshape(devices, width)

    rows = parts * pairs * 3
    state = pltpu.VMEM((rows, LANES), f32)
    ext = pltpu.VMEM(((parts + 2) * elems, 4 * LANES), bf16)
    picked = pltpu.VMEM((rows, 2 * slots * LANES), bf16)
    done = pl.pallas_call(
        functools.partial(solve_kernel, parts, pairs, slots),
        out_shape=jax.ShapeDtypeStruct((parts, comps, pairs, LANES), f32),
        in_specs=[pl.BlockSpec(memory_space=pltpu.SMEM)] + vmem(3), out_specs=vmem(1)[0],
        scratch_shapes=[ext, picked, state, state, state],
        compiler_params=pltpu.CompilerParams(vmem_limit_bytes=24 << 20),
        name="solve",
    )(scal, columns, onehot, weights)
    back = lax.all_to_all(done.reshape(parts, comps * pairs, LANES), "dom", split_axis=0, concat_axis=0, tiled=True)
    back = back.reshape(modes_dev, 2, comps, pairs, LANES).transpose(2, 0, 1, 3, 4)
    return back.reshape(comps, modes_dev, 2, merged)


def solution(mesh):
    placed = (
        P(None, "mode", None, "dom"),
        P(None, "mode", None, "dom"),
        P(),
        P(None, "dom"),
        P(None, "dom"),
    )
    return jax.shard_map(
        shards, mesh=mesh, in_specs=placed, out_specs=P(None, "mode", None, "dom"), check_vma=False
    )
```

```python
import functools

import jax
import jax.numpy as jnp
import numpy as np
from jax import lax
from jax.experimental import pallas as pl
from jax.experimental.pallas import tpu as pltpu
from jax.sharding import PartitionSpec as P


CHEB = 4
UNROLL = 8
NP = 64
COMPS = 3
LANES = 128
bf16, f32 = jnp.bfloat16, jnp.float32


def split(value):
    high = value.astype(bf16)
    return high, (value - high.astype(f32)).astype(bf16)


def np_split(value):
    high = value.astype(np.float32).astype(bf16)
    return high, (value - high.astype(np.float64)).astype(np.float32).astype(bf16)


def spanwise_tables(count, senders):
    planes = 2 * count
    angle = 2 * np.pi / planes * ((np.arange(planes)[:, None] * np.arange(count)[None, :]) % planes)
    weights = np.where(np.arange(count) == 0, 1.0, 2.0)
    forward = np.stack([weights * np.cos(angle), -weights * np.sin(angle)], axis=2).reshape(planes, planes)
    back = np.stack([np.cos(angle).T, -np.sin(angle).T], axis=1).reshape(planes, planes) / planes
    back = back.reshape(senders, -1, planes).swapaxes(0, 1).reshape(planes, planes)
    return np.stack(np_split(forward) + np_split(back))


def dot(a, b):
    return jnp.dot(a, b, preferred_element_type=f32)


def dot3(a, b):
    return dot(a[0], b[0]) + dot(a[1], b[0]) + dot(a[0], b[1])


def pack_kernel(velocity, vorticity, out):
    rows = 2 * velocity.shape[0]
    for i, field in enumerate((velocity, vorticity)):
        for g in range(0, rows, 8):
            value = field[g // 2:g // 2 + 4].reshape(8, field.shape[2])
            for j in range(out.shape[0]):
                out[j, i * rows + g:i * rows + g + 8, :] = value[:, j * LANES:(j + 1) * LANES]


def lines_kernel(lines, tables, out):
    senders, rows, _ = lines.shape
    per = rows // (2 * COMPS)
    count = senders * per
    fields = [lines[:, i * per:(i + 1) * per, :].reshape(count, LANES) for i in range(2 * COMPS)]
    forward = (tables[0], tables[1])
    planes = [dot3(forward, split(jnp.concatenate(fields[i:i + 2], axis=1))) for i in range(0, 2 * COMPS, 2)]
    planes = [half for pair in planes for half in (pair[:, :LANES], pair[:, LANES:])]
    u, w = planes[:COMPS], planes[COMPS:]
    cross = jnp.concatenate([u[(c + 1) % 3] * w[(c + 2) % 3] - u[(c + 2) % 3] * w[(c + 1) % 3] for c in range(3)], axis=1)
    forcing = dot3((tables[2], tables[3]), split(cross))
    row = lax.broadcasted_iota(jnp.int32, (count, LANES), 0)
    mode = (row % senders) * (per // 2) + row // (2 * senders)
    wavenum = mode.astype(f32) * (2.0 / count)
    inv_diag = 1.0 / (1.0 + 4.0 * wavenum * wavenum)
    for c in range(COMPS):
        own = jnp.concatenate([lines[:, c * per + k, :] for k in range(per)], axis=0)
        out[:, 0, c * LANES:(c + 1) * LANES] = (own + forcing[:, c * LANES:(c + 1) * LANES]) * inv_diag


def first_send(slots):
    return -(-2 * slots // 8) * 8


def prep_kernel(parts, pairs, slots, send, order, tables, blocks, onehot, weights, refs_at, kap):
    elems = 2 * pairs
    for k in range(parts):
        refs_at[pl.ds(pl.multiple_of(order[k] * pairs, pairs), pairs), :] = tables[k]

    turned = refs_at[...].T
    first = first_send(slots)
    refs = turned[:first]
    shared = turned[first:first + 2 * send]
    below = pltpu.roll(shared, pairs, 1)
    above = pltpu.roll(shared, (parts - 1) * pairs, 1)
    local = refs
    for s in range(send):
        local = jnp.where(refs == float(elems + s), below[s:s + 1], local)
        local = jnp.where(refs == float(elems + send + s), above[send + s:send + s + 1], local)
    local = local.astype(jnp.int32)
    place = jnp.where(refs < float(elems), elems, jnp.where(refs < float(elems + send), 0, 2 * elems))
    odd = (lax.broadcasted_iota(jnp.int32, place.shape, 1) // pairs) & 1
    place = (place + odd * elems + (local & 1) * pairs + (local >> 1)).astype(f32)
    place = jnp.concatenate([place, jnp.zeros((LANES - first, parts * pairs), f32)], axis=0)
    kap[...] = place.T.astype(jnp.int32)
    lane = lax.broadcasted_iota(jnp.int32, (pairs, LANES), 1)

    def build(d, carry):
        rows = kap[pl.ds(pl.multiple_of(d * pairs, pairs), pairs), :]
        for s in range(slots):
            for h in range(2):
                col = rows[:, h * slots + s:h * slots + s + 1]
                hit = jnp.where(lane == col, 1.0, 0.0).astype(bf16)
                at = pl.multiple_of((d & 1) * slots * elems, elems) + s * elems + h * pairs
                onehot[d >> 1, pl.ds(at, pairs), :] = hit
        return carry

    lax.fori_loop(0, parts, build, 0, unroll=4)

    weights[...] = jnp.zeros_like(weights)

    def place_block(s, carry):
        base = pl.multiple_of(s * LANES, LANES)
        for part, val in enumerate(split(blocks[s].T)):
            for c in range(2):
                at = part * LANES + c * NP
                weights[pl.ds(base + c * NP, NP), at:at + NP] = val
        return carry

    lax.fori_loop(0, slots, place_block, 0, unroll=3)


def solve_kernel(parts, pairs, slots, scal, state_in, onehot, weights, out,
                 ext, picked, sol, resid, dirn):
    elems = 2 * pairs
    ones, twos = parts * pairs, parts * elems
    half = lax.broadcasted_iota(jnp.int32, (ones, LANES), 1) < NP
    few = half[:pairs]
    x = [state_in[:, c * LANES:(c + 1) * LANES] for c in range(COMPS)]
    shape = (parts, pairs, LANES)

    def halves(low, high):
        return jnp.stack([low.reshape(shape), high.reshape(shape)], axis=1).reshape(twos, LANES)

    dirn[:twos] = halves(jnp.where(half, x[0], pltpu.roll(x[1], NP, 1)), jnp.where(half, pltpu.roll(x[0], NP, 1), x[1]))
    dirn[twos:] = x[2]
    resid[...] = dirn[...]
    sol[...] = jnp.zeros_like(sol)
    inv_diag = scal[0]

    def step(i, carry):
        last = dirn[twos:]
        turned = pltpu.roll(last, NP, 1)
        for j, now in enumerate((dirn[:twos], halves(jnp.where(half, last, turned), jnp.where(half, turned, last)))):
            for part, val in enumerate(split(now)):
                lanes = slice((2 * part + j) * LANES, (2 * part + j + 1) * LANES)
                ext[elems:elems + twos, lanes] = val
                ext[:elems, lanes] = val[twos - elems:]
                ext[elems + twos:, lanes] = val[:elems]

        def gather(g, c):
            near = ext[pl.ds(pl.multiple_of(g * 2 * elems, 2 * elems), 4 * elems)]
            window = jnp.concatenate([near[:, :2 * LANES], near[:, 2 * LANES:]], axis=0)
            one = onehot[g]
            for k in range(2):
                this = one[k * slots * elems:(k + 1) * slots * elems]
                y = dot(jnp.concatenate([this, this], axis=1), window)
                two = pl.ds(pl.multiple_of((2 * g + k) * elems, elems), elems)
                single = pl.ds(pl.multiple_of(twos + (2 * g + k) * pairs, pairs), pairs)
                for s in range(slots):
                    row = s * elems
                    both = y[row:row + elems, :LANES]
                    last = y[row:row + elems, LANES:]
                    last = jnp.where(few, last[:pairs], last[pairs:])
                    for at, val in ((two, both), (single, last)):
                        for part, piece in enumerate(split(val)):
                            at_lane = (part * slots + s) * LANES
                            picked[at, at_lane:at_lane + LANES] = piece
            return c

        lax.fori_loop(0, parts // 2, gather, 0, unroll=UNROLL)
        total = dot(picked[...], jnp.concatenate([weights[...], weights[...]], axis=0))
        total = total[:, :LANES] + total[:, LANES:]
        old = dirn[...]
        sol[...] = sol[...] + old
        left = resid[...] - (old + inv_diag * total)
        resid[...] = left
        dirn[...] = scal[1 + 2 * i] * old + scal[2 + 2 * i] * left
        return carry

    lax.fori_loop(0, CHEB, step, 0)
    final = sol[...] + dirn[...]
    both = final[:twos].reshape(parts, 2, pairs, LANES)
    a = [both[:, h].reshape(ones, LANES) for h in range(2)]
    out[:, 0] = jnp.where(half, a[0], pltpu.roll(a[1], NP, 1)).reshape(shape)
    out[:, 1] = jnp.where(half, pltpu.roll(a[0], NP, 1), a[1]).reshape(shape)
    out[:, 2] = final[twos:].reshape(shape)


def vmem(n):
    return [pl.BlockSpec(memory_space=pltpu.VMEM)] * n


def shards(velocity, vorticity, blocks, nbr_ref, send_list):
    comps, modes_dev, _, merged = velocity.shape
    n_mode, parts = lax.axis_size("mode"), lax.axis_size("dom")
    slots, elems = nbr_ref.shape
    send = send_list.shape[1]
    pairs = elems // 2
    modes_all = modes_dev * n_mode
    me = lax.axis_index("mode")
    rows = comps * modes_dev * 2

    packed = pl.pallas_call(
        pack_kernel, out_shape=jax.ShapeDtypeStruct((n_mode, 2 * rows, LANES), f32),
        in_specs=vmem(2), out_specs=vmem(1)[0],
        compiler_params=pltpu.CompilerParams(vmem_limit_bytes=62 << 20), name="pack",
    )(velocity.reshape(comps * modes_dev, 2, merged), vorticity.reshape(comps * modes_dev, 2, merged))
    lines = lax.all_to_all(packed, "mode", split_axis=0, concat_axis=0, tiled=True)

    table = jnp.concatenate([
        nbr_ref.reshape(slots, pairs, 2).transpose(1, 2, 0).reshape(pairs, 2 * slots),
        jnp.zeros((pairs, first_send(slots) - 2 * slots), jnp.int32),
        jnp.broadcast_to(send_list.reshape(1, 2 * send), (pairs, 2 * send)),
    ], axis=1).astype(f32)
    table = jnp.pad(table, ((0, 0), (0, LANES - table.shape[1])))
    side = 4
    here = lax.axis_index("dom")
    near = [lax.ppermute(table, "dom", [(d, d // side * side + (d + i) % side) for d in range(parts)])
            for i in range(1, side)]
    table = jnp.stack([table] + near)
    far = [lax.ppermute(table, "dom", [(d, (d + i * side) % parts) for d in range(parts)])
           for i in range(1, parts // side)]
    table = jnp.concatenate([table] + far, axis=0)
    steps = jnp.arange(parts, dtype=jnp.int32)
    order = (here // side - steps // side) % (parts // side) * side + (here % side - steps % side) % side
    onehot, weights = pl.pallas_call(
        functools.partial(prep_kernel, parts, pairs, slots, send),
        out_shape=[jax.ShapeDtypeStruct((parts // 2, 2 * slots * elems, LANES), bf16),
                   jax.ShapeDtypeStruct((slots * LANES, 2 * LANES), bf16)],
        in_specs=[pl.BlockSpec(memory_space=pltpu.SMEM)] + vmem(2), out_specs=vmem(2),
        scratch_shapes=[pltpu.VMEM((parts * pairs, LANES), f32), pltpu.VMEM((parts * pairs, LANES), jnp.int32)],
        compiler_params=pltpu.CompilerParams(vmem_limit_bytes=8 << 20),
        cost_estimate=pl.CostEstimate(flops=0, bytes_accessed=8 << 20, transcendentals=0),
        name="prep",
    )(order, table, blocks)

    width = comps * LANES
    devices = n_mode * parts
    rhs = pl.pallas_call(
        lines_kernel,
        out_shape=jax.ShapeDtypeStruct((devices, 1, width), f32),
        in_specs=vmem(2), out_specs=vmem(1)[0], name="lines",
        compiler_params=pltpu.CompilerParams(vmem_limit_bytes=12 << 20),
    )(lines, jnp.asarray(spanwise_tables(modes_all, n_mode)))
    mode = me * modes_dev + lax.axis_index("dom") // 2
    wavenum = mode.astype(f32) / modes_all
    coefs = []
    rho = 0.5
    for _ in range(CHEB):
        rho_next = 1.0 / (4.0 - rho)
        coefs += [rho_next * rho, 4.0 * rho_next]
        rho = rho_next
    scal = jnp.concatenate([(1.0 / (1.0 + 4.0 * wavenum * wavenum)).reshape(1), jnp.asarray(coefs, f32)])
    rhs, scal, onehot, weights = lax.optimization_barrier((rhs, scal, onehot, weights))
    columns = lax.all_to_all(rhs, ("dom", "mode"), split_axis=0, concat_axis=0, tiled=True)
    columns = columns.reshape(devices, width)

    rows = parts * pairs * 3
    state = pltpu.VMEM((rows, LANES), f32)
    ext = pltpu.VMEM(((parts + 2) * elems, 4 * LANES), bf16)
    picked = pltpu.VMEM((rows, 2 * slots * LANES), bf16)
    done = pl.pallas_call(
        functools.partial(solve_kernel, parts, pairs, slots),
        out_shape=jax.ShapeDtypeStruct((parts, comps, pairs, LANES), f32),
        in_specs=[pl.BlockSpec(memory_space=pltpu.SMEM)] + vmem(3), out_specs=vmem(1)[0],
        scratch_shapes=[ext, picked, state, state, state],
        compiler_params=pltpu.CompilerParams(vmem_limit_bytes=24 << 20),
        name="solve",
    )(scal, columns, onehot, weights)
    back = lax.all_to_all(done.reshape(parts, comps * pairs, LANES), "dom", split_axis=0, concat_axis=0, tiled=True)
    back = back.reshape(modes_dev, 2, comps, pairs, LANES).transpose(2, 0, 1, 3, 4)
    return back.reshape(comps, modes_dev, 2, merged)


def solution(mesh):
    placed = (
        P(None, "mode", None, "dom"),
        P(None, "mode", None, "dom"),
        P(),
        P(None, "dom"),
        P(None, "dom"),
    )
    return jax.shard_map(
        shards, mesh=mesh, in_specs=placed, out_specs=P(None, "mode", None, "dom"), check_vma=False
    )
```

```python
import functools

import jax
import jax.numpy as jnp
import numpy as np
from jax import lax
from jax.experimental import pallas as pl
from jax.experimental.pallas import tpu as pltpu
from jax.sharding import PartitionSpec as P


CHEB = 4
UNROLL = 8
NP = 64
COMPS = 3
LANES = 128
bf16, f32 = jnp.bfloat16, jnp.float32


def split(value):
    high = value.astype(bf16)
    return high, (value - high.astype(f32)).astype(bf16)


def np_split(value):
    high = value.astype(np.float32).astype(bf16)
    return high, (value - high.astype(np.float64)).astype(np.float32).astype(bf16)


def spanwise_tables(count, senders):
    planes = 2 * count
    angle = 2 * np.pi / planes * ((np.arange(planes)[:, None] * np.arange(count)[None, :]) % planes)
    weights = np.where(np.arange(count) == 0, 1.0, 2.0)
    forward = np.stack([weights * np.cos(angle), -weights * np.sin(angle)], axis=2).reshape(planes, planes)
    back = np.stack([np.cos(angle).T, -np.sin(angle).T], axis=1).reshape(planes, planes) / planes
    back = back.reshape(senders, -1, planes).swapaxes(0, 1).reshape(planes, planes)
    return np.stack(np_split(forward) + np_split(back))


def dot(a, b):
    return jnp.dot(a, b, preferred_element_type=f32)


def dot3(a, b):
    return dot(a[0], b[0]) + dot(a[1], b[0]) + dot(a[0], b[1])


def pack_kernel(velocity, vorticity, out, held, arrived):
    modes = velocity.shape[0] // COMPS
    copies = []
    for i, field in enumerate((velocity, vorticity)):
        for c in range(COMPS):
            at = pl.ds(c * modes, modes)
            copies.append(pltpu.make_async_copy(field.at[at], held.at[i, at], arrived.at[i * COMPS + c]))
            copies[-1].start()
    for i, copy in enumerate(copies):
        copy.wait()
        for g in range(0, modes, 4):
            first = (i % COMPS) * modes + g
            value = held[i // COMPS, first:first + 4].reshape(8, held.shape[3])
            for j in range(out.shape[0]):
                at = 2 * (i * modes + g)
                out[j, at:at + 8, :] = value[:, j * LANES:(j + 1) * LANES]


def lines_kernel(lines, tables, out):
    senders, rows, _ = lines.shape
    per = rows // (2 * COMPS)
    count = senders * per
    fields = [lines[:, i * per:(i + 1) * per, :].reshape(count, LANES) for i in range(2 * COMPS)]
    forward = (tables[0], tables[1])
    planes = [dot3(forward, split(jnp.concatenate(fields[i:i + 2], axis=1))) for i in range(0, 2 * COMPS, 2)]
    planes = [half for pair in planes for half in (pair[:, :LANES], pair[:, LANES:])]
    u, w = planes[:COMPS], planes[COMPS:]
    cross = jnp.concatenate([u[(c + 1) % 3] * w[(c + 2) % 3] - u[(c + 2) % 3] * w[(c + 1) % 3] for c in range(3)], axis=1)
    forcing = dot3((tables[2], tables[3]), split(cross))
    row = lax.broadcasted_iota(jnp.int32, (count, LANES), 0)
    mode = (row % senders) * (per // 2) + row // (2 * senders)
    wavenum = mode.astype(f32) * (2.0 / count)
    inv_diag = 1.0 / (1.0 + 4.0 * wavenum * wavenum)
    for c in range(COMPS):
        own = jnp.concatenate([lines[:, c * per + k, :] for k in range(per)], axis=0)
        out[:, 0, c * LANES:(c + 1) * LANES] = (own + forcing[:, c * LANES:(c + 1) * LANES]) * inv_diag


def first_send(slots):
    return -(-2 * slots // 8) * 8


def prep_kernel(parts, pairs, slots, send, order, tables, blocks, onehot, weights, refs_at, kap):
    elems = 2 * pairs
    for k in range(parts):
        refs_at[pl.ds(pl.multiple_of(order[k] * pairs, pairs), pairs), :] = tables[k]

    turned = refs_at[...].T
    first = first_send(slots)
    refs = turned[:first]
    shared = turned[first:first + 2 * send]
    below = pltpu.roll(shared, pairs, 1)
    above = pltpu.roll(shared, (parts - 1) * pairs, 1)
    local = refs
    for s in range(send):
        local = jnp.where(refs == float(elems + s), below[s:s + 1], local)
        local = jnp.where(refs == float(elems + send + s), above[send + s:send + s + 1], local)
    local = local.astype(jnp.int32)
    place = jnp.where(refs < float(elems), elems, jnp.where(refs < float(elems + send), 0, 2 * elems))
    odd = (lax.broadcasted_iota(jnp.int32, place.shape, 1) // pairs) & 1
    place = (place + odd * elems + (local & 1) * pairs + (local >> 1)).astype(f32)
    place = jnp.concatenate([place, jnp.zeros((LANES - first, parts * pairs), f32)], axis=0)
    kap[...] = place.T.astype(jnp.int32)
    lane = lax.broadcasted_iota(jnp.int32, (pairs, LANES), 1)

    def build(d, carry):
        rows = kap[pl.ds(pl.multiple_of(d * pairs, pairs), pairs), :]
        for s in range(slots):
            for h in range(2):
                col = rows[:, h * slots + s:h * slots + s + 1]
                hit = jnp.where(lane == col, 1.0, 0.0).astype(bf16)
                at = pl.multiple_of((d & 1) * slots * elems, elems) + s * elems + h * pairs
                onehot[d >> 1, pl.ds(at, pairs), :] = hit
        return carry

    lax.fori_loop(0, parts, build, 0, unroll=4)

    weights[...] = jnp.zeros_like(weights)

    def place_block(s, carry):
        base = pl.multiple_of(s * LANES, LANES)
        for part, val in enumerate(split(blocks[s].T)):
            for c in range(2):
                at = part * LANES + c * NP
                weights[pl.ds(base + c * NP, NP), at:at + NP] = val
        return carry

    lax.fori_loop(0, slots, place_block, 0, unroll=3)


def solve_kernel(parts, pairs, slots, scal, state_in, onehot, weights, out,
                 ext, picked, sol, resid, dirn):
    elems = 2 * pairs
    ones, twos = parts * pairs, parts * elems
    half = lax.broadcasted_iota(jnp.int32, (ones, LANES), 1) < NP
    few = half[:pairs]
    x = [state_in[:, c * LANES:(c + 1) * LANES] for c in range(COMPS)]
    shape = (parts, pairs, LANES)

    def halves(low, high):
        return jnp.stack([low.reshape(shape), high.reshape(shape)], axis=1).reshape(twos, LANES)

    dirn[:twos] = halves(jnp.where(half, x[0], pltpu.roll(x[1], NP, 1)), jnp.where(half, pltpu.roll(x[0], NP, 1), x[1]))
    dirn[twos:] = x[2]
    resid[...] = dirn[...]
    sol[...] = jnp.zeros_like(sol)
    inv_diag = scal[0]

    def step(i, carry):
        last = dirn[twos:]
        turned = pltpu.roll(last, NP, 1)
        for j, now in enumerate((dirn[:twos], halves(jnp.where(half, last, turned), jnp.where(half, turned, last)))):
            for part, val in enumerate(split(now)):
                lanes = slice((2 * part + j) * LANES, (2 * part + j + 1) * LANES)
                ext[elems:elems + twos, lanes] = val
                ext[:elems, lanes] = val[twos - elems:]
                ext[elems + twos:, lanes] = val[:elems]

        def gather(g, c):
            near = ext[pl.ds(pl.multiple_of(g * 2 * elems, 2 * elems), 4 * elems)]
            window = jnp.concatenate([near[:, :2 * LANES], near[:, 2 * LANES:]], axis=0)
            one = onehot[g]
            for k in range(2):
                this = one[k * slots * elems:(k + 1) * slots * elems]
                y = dot(jnp.concatenate([this, this], axis=1), window)
                two = pl.ds(pl.multiple_of((2 * g + k) * elems, elems), elems)
                single = pl.ds(pl.multiple_of(twos + (2 * g + k) * pairs, pairs), pairs)
                for s in range(slots):
                    row = s * elems
                    both = y[row:row + elems, :LANES]
                    last = y[row:row + elems, LANES:]
                    last = jnp.where(few, last[:pairs], last[pairs:])
                    for at, val in ((two, both), (single, last)):
                        for part, piece in enumerate(split(val)):
                            at_lane = (part * slots + s) * LANES
                            picked[at, at_lane:at_lane + LANES] = piece
            return c

        lax.fori_loop(0, parts // 2, gather, 0, unroll=UNROLL)
        total = dot(picked[...], jnp.concatenate([weights[...], weights[...]], axis=0))
        total = total[:, :LANES] + total[:, LANES:]
        old = dirn[...]
        sol[...] = sol[...] + old
        left = resid[...] - (old + inv_diag * total)
        resid[...] = left
        dirn[...] = scal[1 + 2 * i] * old + scal[2 + 2 * i] * left
        return carry

    lax.fori_loop(0, CHEB, step, 0)
    final = sol[...] + dirn[...]
    both = final[:twos].reshape(parts, 2, pairs, LANES)
    a = [both[:, h].reshape(ones, LANES) for h in range(2)]
    out[:, 0] = jnp.where(half, a[0], pltpu.roll(a[1], NP, 1)).reshape(shape)
    out[:, 1] = jnp.where(half, pltpu.roll(a[0], NP, 1), a[1]).reshape(shape)
    out[:, 2] = final[twos:].reshape(shape)


def vmem(n):
    return [pl.BlockSpec(memory_space=pltpu.VMEM)] * n


def shards(velocity, vorticity, blocks, nbr_ref, send_list):
    comps, modes_dev, _, merged = velocity.shape
    n_mode, parts = lax.axis_size("mode"), lax.axis_size("dom")
    slots, elems = nbr_ref.shape
    send = send_list.shape[1]
    pairs = elems // 2
    modes_all = modes_dev * n_mode
    me = lax.axis_index("mode")
    rows = comps * modes_dev * 2

    packed = pl.pallas_call(
        pack_kernel, out_shape=jax.ShapeDtypeStruct((n_mode, 2 * rows, LANES), f32),
        in_specs=[pl.BlockSpec(memory_space=pl.ANY)] * 2, out_specs=vmem(1)[0],
        scratch_shapes=[pltpu.VMEM((2, comps * modes_dev, 2, merged), f32), pltpu.SemaphoreType.DMA((2 * comps,))],
        compiler_params=pltpu.CompilerParams(vmem_limit_bytes=62 << 20), name="pack",
    )(velocity.reshape(comps * modes_dev, 2, merged), vorticity.reshape(comps * modes_dev, 2, merged))
    lines = lax.all_to_all(packed.reshape(n_mode, 1, 2 * rows * LANES), "mode", split_axis=0, concat_axis=0, tiled=True)
    lines = lines.reshape(packed.shape)

    table = jnp.concatenate([
        nbr_ref.reshape(slots, pairs, 2).transpose(1, 2, 0).reshape(pairs, 2 * slots),
        jnp.zeros((pairs, first_send(slots) - 2 * slots), jnp.int32),
        jnp.broadcast_to(send_list.reshape(1, 2 * send), (pairs, 2 * send)),
    ], axis=1).astype(f32)
    table = jnp.pad(table, ((0, 0), (0, LANES - table.shape[1])))
    side = 4
    here = lax.axis_index("dom")
    near = [lax.ppermute(table, "dom", [(d, d // side * side + (d + i) % side) for d in range(parts)])
            for i in range(1, side)]
    table = jnp.stack([table] + near)
    far = [lax.ppermute(table, "dom", [(d, (d + i * side) % parts) for d in range(parts)])
           for i in range(1, parts // side)]
    table = jnp.concatenate([table] + far, axis=0)
    steps = jnp.arange(parts, dtype=jnp.int32)
    order = (here // side - steps // side) % (parts // side) * side + (here % side - steps % side) % side
    onehot, weights = pl.pallas_call(
        functools.partial(prep_kernel, parts, pairs, slots, send),
        out_shape=[jax.ShapeDtypeStruct((parts // 2, 2 * slots * elems, LANES), bf16),
                   jax.ShapeDtypeStruct((slots * LANES, 2 * LANES), bf16)],
        in_specs=[pl.BlockSpec(memory_space=pltpu.SMEM)] + vmem(2), out_specs=vmem(2),
        scratch_shapes=[pltpu.VMEM((parts * pairs, LANES), f32), pltpu.VMEM((parts * pairs, LANES), jnp.int32)],
        compiler_params=pltpu.CompilerParams(vmem_limit_bytes=8 << 20),
        cost_estimate=pl.CostEstimate(flops=0, bytes_accessed=8 << 20, transcendentals=0),
        name="prep",
    )(order, table, blocks)

    width = comps * LANES
    devices = n_mode * parts
    rhs = pl.pallas_call(
        lines_kernel,
        out_shape=jax.ShapeDtypeStruct((devices, 1, width), f32),
        in_specs=vmem(2), out_specs=vmem(1)[0], name="lines",
        compiler_params=pltpu.CompilerParams(vmem_limit_bytes=12 << 20),
    )(lines, jnp.asarray(spanwise_tables(modes_all, n_mode)))
    mode = me * modes_dev + lax.axis_index("dom") // 2
    wavenum = mode.astype(f32) / modes_all
    coefs = []
    rho = 0.5
    for _ in range(CHEB):
        rho_next = 1.0 / (4.0 - rho)
        coefs += [rho_next * rho, 4.0 * rho_next]
        rho = rho_next
    scal = jnp.concatenate([(1.0 / (1.0 + 4.0 * wavenum * wavenum)).reshape(1), jnp.asarray(coefs, f32)])
    rhs, scal, onehot, weights = lax.optimization_barrier((rhs, scal, onehot, weights))
    columns = lax.all_to_all(rhs, ("dom", "mode"), split_axis=0, concat_axis=0, tiled=True)
    columns = columns.reshape(devices, width)

    rows = parts * pairs * 3
    state = pltpu.VMEM((rows, LANES), f32)
    ext = pltpu.VMEM(((parts + 2) * elems, 4 * LANES), bf16)
    picked = pltpu.VMEM((rows, 2 * slots * LANES), bf16)
    done = pl.pallas_call(
        functools.partial(solve_kernel, parts, pairs, slots),
        out_shape=jax.ShapeDtypeStruct((parts, comps, pairs, LANES), f32),
        in_specs=[pl.BlockSpec(memory_space=pltpu.SMEM)] + vmem(3), out_specs=vmem(1)[0],
        scratch_shapes=[ext, picked, state, state, state],
        compiler_params=pltpu.CompilerParams(
            vmem_limit_bytes=24 << 20),
        name="solve",
    )(scal, columns, onehot, weights)
    back = lax.all_to_all(done.reshape(parts, 1, comps * pairs * LANES), "dom", split_axis=0, concat_axis=0, tiled=True)
    back = back.reshape(modes_dev, 2, comps, pairs, LANES).transpose(2, 0, 1, 3, 4)
    return back.reshape(comps, modes_dev, 2, merged)


def solution(mesh):
    placed = (
        P(None, "mode", None, "dom"),
        P(None, "mode", None, "dom"),
        P(),
        P(None, "dom"),
        P(None, "dom"),
    )
    return jax.shard_map(
        shards, mesh=mesh, in_specs=placed, out_specs=P(None, "mode", None, "dom"), check_vma=False
    )
```

```python
import functools

import jax
import jax.numpy as jnp
import numpy as np
from jax import lax
from jax.experimental import pallas as pl
from jax.experimental.pallas import tpu as pltpu
from jax.sharding import PartitionSpec as P


CHEB = 4
UNROLL = 8
NP = 64
COMPS = 3
LANES = 128
bf16, f32 = jnp.bfloat16, jnp.float32


def split(value):
    high = value.astype(bf16)
    return high, (value - high.astype(f32)).astype(bf16)


def np_split(value):
    high = value.astype(np.float32).astype(bf16)
    return high, (value - high.astype(np.float64)).astype(np.float32).astype(bf16)


def spanwise_tables(count, senders):
    planes = 2 * count
    angle = 2 * np.pi / planes * ((np.arange(planes)[:, None] * np.arange(count)[None, :]) % planes)
    weights = np.where(np.arange(count) == 0, 1.0, 2.0)
    forward = np.stack([weights * np.cos(angle), -weights * np.sin(angle)], axis=2).reshape(planes, planes)
    back = np.stack([np.cos(angle).T, -np.sin(angle).T], axis=1).reshape(planes, planes) / planes
    back = back.reshape(senders, -1, planes).swapaxes(0, 1).reshape(planes, planes)
    return np.stack(np_split(forward) + np_split(back))


def dot(a, b):
    return jnp.dot(a, b, preferred_element_type=f32)


def dot3(a, b):
    return dot(a[0], b[0]) + dot(a[1], b[0]) + dot(a[0], b[1])


def pack_kernel(velocity, vorticity, out, held, arrived):
    modes = velocity.shape[0] // COMPS
    copies = []
    for i, field in enumerate((velocity, vorticity)):
        for c in range(COMPS):
            at = pl.ds(c * modes, modes)
            copies.append(pltpu.make_async_copy(field.at[at], held.at[i, at], arrived.at[i * COMPS + c]))
            copies[-1].start()
    for i, copy in enumerate(copies):
        copy.wait()
        for g in range(0, modes, 4):
            first = (i % COMPS) * modes + g
            value = held[i // COMPS, first:first + 4].reshape(8, held.shape[3])
            for j in range(out.shape[0]):
                at = 2 * (i * modes + g)
                out[j, at:at + 8, :] = value[:, j * LANES:(j + 1) * LANES]


def lines_kernel(lines, tables, out):
    senders, rows, _ = lines.shape
    per = rows // (2 * COMPS)
    count = senders * per
    fields = [lines[:, i * per:(i + 1) * per, :].reshape(count, LANES) for i in range(2 * COMPS)]
    forward = (tables[0], tables[1])
    planes = [dot3(forward, split(jnp.concatenate(fields[i:i + 2], axis=1))) for i in range(0, 2 * COMPS, 2)]
    planes = [half for pair in planes for half in (pair[:, :LANES], pair[:, LANES:])]
    u, w = planes[:COMPS], planes[COMPS:]
    cross = jnp.concatenate([u[(c + 1) % 3] * w[(c + 2) % 3] - u[(c + 2) % 3] * w[(c + 1) % 3] for c in range(3)], axis=1)
    forcing = dot3((tables[2], tables[3]), split(cross))
    row = lax.broadcasted_iota(jnp.int32, (count, LANES), 0)
    mode = (row % senders) * (per // 2) + row // (2 * senders)
    wavenum = mode.astype(f32) * (2.0 / count)
    inv_diag = 1.0 / (1.0 + 4.0 * wavenum * wavenum)
    for c in range(COMPS):
        own = jnp.concatenate([lines[:, c * per + k, :] for k in range(per)], axis=0)
        out[:, 0, c * LANES:(c + 1) * LANES] = (own + forcing[:, c * LANES:(c + 1) * LANES]) * inv_diag


def first_send(slots):
    return -(-2 * slots // 8) * 8


def prep_kernel(parts, pairs, slots, send, order, *refs):
    *tables, onehot, refs_at, kap = refs
    elems = 2 * pairs
    side = parts // len(tables)
    for k in range(parts):
        refs_at[pl.ds(pl.multiple_of(order[k] * pairs, pairs), pairs), :] = tables[k // side][k % side]

    turned = refs_at[...].T
    first = first_send(slots)
    refs = turned[:first]
    shared = turned[first:first + 2 * send]
    below = pltpu.roll(shared, pairs, 1)
    above = pltpu.roll(shared, (parts - 1) * pairs, 1)
    local = refs
    for s in range(send):
        local = jnp.where(refs == float(elems + s), below[s:s + 1], local)
        local = jnp.where(refs == float(elems + send + s), above[send + s:send + s + 1], local)
    local = local.astype(jnp.int32)
    place = jnp.where(refs < float(elems), elems, jnp.where(refs < float(elems + send), 0, 2 * elems))
    odd = (lax.broadcasted_iota(jnp.int32, place.shape, 1) // pairs) & 1
    place = (place + odd * elems + (local & 1) * pairs + (local >> 1)).astype(f32)
    place = jnp.concatenate([place, jnp.zeros((LANES - first, parts * pairs), f32)], axis=0)
    kap[...] = place.T.astype(jnp.int32)
    lane = lax.broadcasted_iota(jnp.int32, (pairs, LANES), 1)

    def build(d, carry):
        rows = kap[pl.ds(pl.multiple_of(d * pairs, pairs), pairs), :]
        for s in range(slots):
            for h in range(2):
                col = rows[:, h * slots + s:h * slots + s + 1]
                hit = jnp.where(lane == col, 1.0, 0.0).astype(bf16)
                at = pl.multiple_of((d & 1) * slots * elems, elems) + s * elems + h * pairs
                onehot[d >> 1, pl.ds(at, pairs), :] = hit
        return carry

    lax.fori_loop(0, parts, build, 0, unroll=parts)


def weight_kernel(slots, blocks, weights):
    weights[...] = jnp.zeros_like(weights)

    def place_block(s, carry):
        base = pl.multiple_of(s * LANES, LANES)
        for part, val in enumerate(split(blocks[s].T)):
            for c in range(2):
                at = part * LANES + c * NP
                weights[pl.ds(base + c * NP, NP), at:at + NP] = val
        return carry

    lax.fori_loop(0, slots, place_block, 0, unroll=slots)


def solve_kernel(parts, pairs, slots, scal, state_in, onehot, weights, out,
                 ext, picked, sol, resid, dirn):
    elems = 2 * pairs
    ones, twos = parts * pairs, parts * elems
    half = lax.broadcasted_iota(jnp.int32, (ones, LANES), 1) < NP
    few = half[:pairs]
    x = [state_in[:, c * LANES:(c + 1) * LANES] for c in range(COMPS)]
    shape = (parts, pairs, LANES)

    def halves(low, high):
        return jnp.stack([low.reshape(shape), high.reshape(shape)], axis=1).reshape(twos, LANES)

    dirn[:twos] = halves(jnp.where(half, x[0], pltpu.roll(x[1], NP, 1)), jnp.where(half, pltpu.roll(x[0], NP, 1), x[1]))
    dirn[twos:] = x[2]
    resid[...] = dirn[...]
    sol[...] = jnp.zeros_like(sol)
    inv_diag = scal[0]

    def step(i, carry):
        last = dirn[twos:]
        turned = pltpu.roll(last, NP, 1)
        for j, now in enumerate((dirn[:twos], halves(jnp.where(half, last, turned), jnp.where(half, turned, last)))):
            for part, val in enumerate(split(now)):
                lanes = slice((2 * part + j) * LANES, (2 * part + j + 1) * LANES)
                ext[elems:elems + twos, lanes] = val
                ext[:elems, lanes] = val[twos - elems:]
                ext[elems + twos:, lanes] = val[:elems]

        def gather(g, c):
            near = ext[pl.ds(pl.multiple_of(g * 2 * elems, 2 * elems), 4 * elems)]
            window = jnp.concatenate([near[:, :2 * LANES], near[:, 2 * LANES:]], axis=0)
            one = onehot[g]
            for k in range(2):
                this = one[k * slots * elems:(k + 1) * slots * elems]
                y = dot(jnp.concatenate([this, this], axis=1), window)
                two = pl.ds(pl.multiple_of((2 * g + k) * elems, elems), elems)
                single = pl.ds(pl.multiple_of(twos + (2 * g + k) * pairs, pairs), pairs)
                for s in range(slots):
                    row = s * elems
                    both = y[row:row + elems, :LANES]
                    last = y[row:row + elems, LANES:]
                    last = jnp.where(few, last[:pairs], last[pairs:])
                    for at, val in ((two, both), (single, last)):
                        for part, piece in enumerate(split(val)):
                            at_lane = (part * slots + s) * LANES
                            picked[at, at_lane:at_lane + LANES] = piece
            return c

        lax.fori_loop(0, parts // 2, gather, 0, unroll=UNROLL)
        total = dot(picked[...], jnp.concatenate([weights[...], weights[...]], axis=0))
        total = total[:, :LANES] + total[:, LANES:]
        old = dirn[...]
        sol[...] = sol[...] + old
        left = resid[...] - (old + inv_diag * total)
        resid[...] = left
        dirn[...] = scal[1 + 2 * i] * old + scal[2 + 2 * i] * left
        return carry

    lax.fori_loop(0, CHEB, step, 0)
    final = sol[...] + dirn[...]
    both = final[:twos].reshape(parts, 2, pairs, LANES)
    a = [both[:, h].reshape(ones, LANES) for h in range(2)]
    out[:, 0] = jnp.where(half, a[0], pltpu.roll(a[1], NP, 1)).reshape(shape)
    out[:, 1] = jnp.where(half, pltpu.roll(a[0], NP, 1), a[1]).reshape(shape)
    out[:, 2] = final[twos:].reshape(shape)


def vmem(n):
    return [pl.BlockSpec(memory_space=pltpu.VMEM)] * n


def shards(velocity, vorticity, blocks, nbr_ref, send_list):
    comps, modes_dev, _, merged = velocity.shape
    n_mode, parts = lax.axis_size("mode"), lax.axis_size("dom")
    slots, elems = nbr_ref.shape
    send = send_list.shape[1]
    pairs = elems // 2
    modes_all = modes_dev * n_mode
    me = lax.axis_index("mode")
    rows = comps * modes_dev * 2

    packed = pl.pallas_call(
        pack_kernel, out_shape=jax.ShapeDtypeStruct((n_mode, 2 * rows, LANES), f32),
        in_specs=[pl.BlockSpec(memory_space=pl.ANY)] * 2, out_specs=vmem(1)[0],
        scratch_shapes=[pltpu.VMEM((2, comps * modes_dev, 2, merged), f32), pltpu.SemaphoreType.DMA((2 * comps,))],
        compiler_params=pltpu.CompilerParams(vmem_limit_bytes=62 << 20), name="pack",
    )(velocity.reshape(comps * modes_dev, 2, merged), vorticity.reshape(comps * modes_dev, 2, merged))
    lines = lax.all_to_all(packed.reshape(n_mode, 1, 2 * rows * LANES), "mode", split_axis=0, concat_axis=0, tiled=True)
    lines = lines.reshape(packed.shape)

    table = jnp.concatenate([
        nbr_ref.reshape(slots, pairs, 2).transpose(1, 2, 0).reshape(pairs, 2 * slots),
        jnp.zeros((pairs, first_send(slots) - 2 * slots), jnp.int32),
        jnp.broadcast_to(send_list.reshape(1, 2 * send), (pairs, 2 * send)),
    ], axis=1).astype(f32)
    table = jnp.pad(table, ((0, 0), (0, LANES - table.shape[1])))
    side = 4
    here = lax.axis_index("dom")
    near = [lax.ppermute(table, "dom", [(d, d // side * side + (d + i) % side) for d in range(parts)])
            for i in range(1, side)]
    table = jnp.stack([table] + near)
    far = [lax.ppermute(table, "dom", [(d, (d + i * side) % parts) for d in range(parts)])
           for i in range(1, parts // side)]
    tables = [table] + far
    steps = jnp.arange(parts, dtype=jnp.int32)
    order = (here // side - steps // side) % (parts // side) * side + (here % side - steps % side) % side
    onehot = pl.pallas_call(
        functools.partial(prep_kernel, parts, pairs, slots, send),
        out_shape=jax.ShapeDtypeStruct((parts // 2, 2 * slots * elems, LANES), bf16),
        in_specs=[pl.BlockSpec(memory_space=pltpu.SMEM)] + vmem(len(tables)), out_specs=vmem(1)[0],
        scratch_shapes=[pltpu.VMEM((parts * pairs, LANES), f32), pltpu.VMEM((parts * pairs, LANES), jnp.int32)],
        compiler_params=pltpu.CompilerParams(vmem_limit_bytes=8 << 20),
        cost_estimate=pl.CostEstimate(flops=0, bytes_accessed=8 << 20, transcendentals=0),
        name="prep",
    )(order, *tables)
    weights = pl.pallas_call(
        functools.partial(weight_kernel, slots),
        out_shape=jax.ShapeDtypeStruct((slots * LANES, 2 * LANES), bf16),
        in_specs=vmem(1), out_specs=vmem(1)[0],
        compiler_params=pltpu.CompilerParams(vmem_limit_bytes=4 << 20),
        cost_estimate=pl.CostEstimate(flops=0, bytes_accessed=1 << 20, transcendentals=0),
        name="weights",
    )(blocks)

    width = comps * LANES
    devices = n_mode * parts
    rhs = pl.pallas_call(
        lines_kernel,
        out_shape=jax.ShapeDtypeStruct((devices, 1, width), f32),
        in_specs=vmem(2), out_specs=vmem(1)[0], name="lines",
        compiler_params=pltpu.CompilerParams(vmem_limit_bytes=12 << 20),
    )(lines, jnp.asarray(spanwise_tables(modes_all, n_mode)))
    mode = me * modes_dev + lax.axis_index("dom") // 2
    wavenum = mode.astype(f32) / modes_all
    coefs = []
    rho = 0.5
    for _ in range(CHEB):
        rho_next = 1.0 / (4.0 - rho)
        coefs += [rho_next * rho, 4.0 * rho_next]
        rho = rho_next
    scal = jnp.concatenate([(1.0 / (1.0 + 4.0 * wavenum * wavenum)).reshape(1), jnp.asarray(coefs, f32)])
    rhs, scal, onehot, weights = lax.optimization_barrier((rhs, scal, onehot, weights))
    columns = lax.all_to_all(rhs, ("dom", "mode"), split_axis=0, concat_axis=0, tiled=True)
    columns = columns.reshape(devices, width)

    rows = parts * pairs * 3
    state = pltpu.VMEM((rows, LANES), f32)
    ext = pltpu.VMEM(((parts + 2) * elems, 4 * LANES), bf16)
    picked = pltpu.VMEM((rows, 2 * slots * LANES), bf16)
    done = pl.pallas_call(
        functools.partial(solve_kernel, parts, pairs, slots),
        out_shape=jax.ShapeDtypeStruct((parts, comps, pairs, LANES), f32),
        in_specs=[pl.BlockSpec(memory_space=pltpu.SMEM)] + vmem(3), out_specs=vmem(1)[0],
        scratch_shapes=[ext, picked, state, state, state],
        compiler_params=pltpu.CompilerParams(
            vmem_limit_bytes=24 << 20),
        name="solve",
    )(scal, columns, onehot, weights)
    back = lax.all_to_all(done.reshape(parts, 1, comps * pairs * LANES), "dom", split_axis=0, concat_axis=0, tiled=True)
    back = back.reshape(modes_dev, 2, comps, pairs, LANES).transpose(2, 0, 1, 3, 4)
    return back.reshape(comps, modes_dev, 2, merged)


def solution(mesh):
    placed = (
        P(None, "mode", None, "dom"),
        P(None, "mode", None, "dom"),
        P(),
        P(None, "dom"),
        P(None, "dom"),
    )
    return jax.shard_map(
        shards, mesh=mesh, in_specs=placed, out_specs=P(None, "mode", None, "dom"), check_vma=False
    )
```

```python
import functools

import jax
import jax.numpy as jnp
import numpy as np
from jax import lax
from jax.experimental import pallas as pl
from jax.experimental.pallas import tpu as pltpu
from jax.sharding import PartitionSpec as P


CHEB = 4
UNROLL = 8
NP = 64
COMPS = 3
LANES = 128
bf16, f32 = jnp.bfloat16, jnp.float32


def split(value):
    high = value.astype(bf16)
    return high, (value - high.astype(f32)).astype(bf16)


def np_split(value):
    high = value.astype(np.float32).astype(bf16)
    return high, (value - high.astype(np.float64)).astype(np.float32).astype(bf16)


def spanwise_tables(count, senders):
    planes = 2 * count
    angle = 2 * np.pi / planes * ((np.arange(planes)[:, None] * np.arange(count)[None, :]) % planes)
    weights = np.where(np.arange(count) == 0, 1.0, 2.0)
    forward = np.stack([weights * np.cos(angle), -weights * np.sin(angle)], axis=2).reshape(planes, planes)
    back = np.stack([np.cos(angle).T, -np.sin(angle).T], axis=1).reshape(planes, planes) / planes
    back = back.reshape(senders, -1, planes).swapaxes(0, 1).reshape(planes, planes)
    return np.stack(np_split(forward) + np_split(back))


def dot(a, b):
    return jnp.dot(a, b, preferred_element_type=f32)


def dot3(a, b):
    return dot(a[0], b[0]) + dot(a[1], b[0]) + dot(a[0], b[1])


def pack_kernel(velocity, vorticity, out, held, arrived):
    modes = velocity.shape[0] // COMPS
    copies = []
    for i, field in enumerate((velocity, vorticity)):
        for c in range(COMPS):
            at = pl.ds(c * modes, modes)
            copies.append(pltpu.make_async_copy(field.at[at], held.at[i, at], arrived.at[i * COMPS + c]))
            copies[-1].start()
    for i, copy in enumerate(copies):
        copy.wait()
        for g in range(0, modes, 4):
            first = (i % COMPS) * modes + g
            value = held[i // COMPS, first:first + 4].reshape(8, held.shape[3])
            for j in range(out.shape[0]):
                at = 2 * (i * modes + g)
                out[j, at:at + 8, :] = value[:, j * LANES:(j + 1) * LANES]


def lines_kernel(lines, tables, out):
    senders, rows, _ = lines.shape
    per = rows // (2 * COMPS)
    count = senders * per
    fields = [lines[:, i * per:(i + 1) * per, :].reshape(count, LANES) for i in range(2 * COMPS)]
    forward = (tables[0], tables[1])
    planes = [dot3(forward, split(jnp.concatenate(fields[i:i + 2], axis=1))) for i in range(0, 2 * COMPS, 2)]
    planes = [half for pair in planes for half in (pair[:, :LANES], pair[:, LANES:])]
    u, w = planes[:COMPS], planes[COMPS:]
    cross = jnp.concatenate([u[(c + 1) % 3] * w[(c + 2) % 3] - u[(c + 2) % 3] * w[(c + 1) % 3] for c in range(3)], axis=1)
    forcing = dot3((tables[2], tables[3]), split(cross))
    row = lax.broadcasted_iota(jnp.int32, (count, LANES), 0)
    mode = (row % senders) * (per // 2) + row // (2 * senders)
    wavenum = mode.astype(f32) * (2.0 / count)
    inv_diag = 1.0 / (1.0 + 4.0 * wavenum * wavenum)
    for c in range(COMPS):
        own = jnp.concatenate([lines[:, c * per + k, :] for k in range(per)], axis=0)
        out[:, 0, c * LANES:(c + 1) * LANES] = (own + forcing[:, c * LANES:(c + 1) * LANES]) * inv_diag


def first_send(slots):
    return -(-2 * slots // 8) * 8


def prep_kernel(parts, pairs, slots, send, order, *refs):
    *tables, onehot, refs_at, kap = refs
    elems = 2 * pairs
    side = parts // len(tables)
    for k in range(parts):
        refs_at[pl.ds(pl.multiple_of(order[k] * pairs, pairs), pairs), :] = tables[k // side][k % side]

    turned = refs_at[...].T
    first = first_send(slots)
    refs = turned[:first]
    shared = turned[first:first + 2 * send]
    below = pltpu.roll(shared, pairs, 1)
    above = pltpu.roll(shared, (parts - 1) * pairs, 1)
    local = refs
    for s in range(send):
        local = jnp.where(refs == float(elems + s), below[s:s + 1], local)
        local = jnp.where(refs == float(elems + send + s), above[send + s:send + s + 1], local)
    local = local.astype(jnp.int32)
    place = jnp.where(refs < float(elems), elems, jnp.where(refs < float(elems + send), 0, 2 * elems))
    odd = (lax.broadcasted_iota(jnp.int32, place.shape, 1) // pairs) & 1
    place = (place + odd * elems + (local & 1) * pairs + (local >> 1)).astype(f32)
    place = jnp.concatenate([place, jnp.zeros((LANES - first, parts * pairs), f32)], axis=0)
    kap[...] = place.T.astype(jnp.int32)
    lane = lax.broadcasted_iota(jnp.int32, (pairs, LANES), 1)

    def build(d, carry):
        rows = kap[pl.ds(pl.multiple_of(d * pairs, pairs), pairs), :]
        for s in range(slots):
            for h in range(2):
                col = rows[:, h * slots + s:h * slots + s + 1]
                hit = jnp.where(lane == col, 1.0, 0.0).astype(bf16)
                at = pl.multiple_of((d & 1) * slots * elems, elems) + s * elems + h * pairs
                onehot[d >> 1, pl.ds(at, pairs), :] = hit
        return carry

    lax.fori_loop(0, parts, build, 0, unroll=parts)


def weight_kernel(slots, blocks, weights):
    weights[...] = jnp.zeros_like(weights)

    def place_block(s, carry):
        base = pl.multiple_of(s * LANES, LANES)
        for part, val in enumerate(split(blocks[s].T)):
            for c in range(2):
                at = part * LANES + c * NP
                weights[pl.ds(base + c * NP, NP), at:at + NP] = val
        return carry

    lax.fori_loop(0, slots, place_block, 0, unroll=slots)


def solve_kernel(parts, pairs, slots, scal, state_in, onehot, weights, out,
                 ext, picked, sol, resid, dirn):
    elems = 2 * pairs
    ones, twos = parts * pairs, parts * elems
    half = lax.broadcasted_iota(jnp.int32, (ones, LANES), 1) < NP
    few = half[:pairs]
    x = [state_in[:, c * LANES:(c + 1) * LANES] for c in range(COMPS)]
    shape = (parts, pairs, LANES)

    def halves(low, high):
        return jnp.stack([low.reshape(shape), high.reshape(shape)], axis=1).reshape(twos, LANES)

    dirn[:twos] = halves(jnp.where(half, x[0], pltpu.roll(x[1], NP, 1)), jnp.where(half, pltpu.roll(x[0], NP, 1), x[1]))
    dirn[twos:] = x[2]
    resid[...] = dirn[...]
    sol[...] = dirn[...]
    inv_diag = scal[0]

    def step(i, carry):
        last = dirn[twos:]
        turned = pltpu.roll(last, NP, 1)
        for j, now in enumerate((dirn[:twos], halves(jnp.where(half, last, turned), jnp.where(half, turned, last)))):
            for part, val in enumerate(split(now)):
                lanes = slice((2 * part + j) * LANES, (2 * part + j + 1) * LANES)
                ext[elems:elems + twos, lanes] = val
                ext[:elems, lanes] = val[twos - elems:]
                ext[elems + twos:, lanes] = val[:elems]

        def gather(g, c):
            near = ext[pl.ds(pl.multiple_of(g * 2 * elems, 2 * elems), 4 * elems)]
            window = jnp.concatenate([near[:, :2 * LANES], near[:, 2 * LANES:]], axis=0)
            one = onehot[g]
            for k in range(2):
                this = one[k * slots * elems:(k + 1) * slots * elems]
                y = dot(jnp.concatenate([this, this], axis=1), window)
                two = pl.ds(pl.multiple_of((2 * g + k) * elems, elems), elems)
                single = pl.ds(pl.multiple_of(twos + (2 * g + k) * pairs, pairs), pairs)
                for s in range(slots):
                    row = s * elems
                    both = y[row:row + elems, :LANES]
                    last = y[row:row + elems, LANES:]
                    last = jnp.where(few, last[:pairs], last[pairs:])
                    for at, val in ((two, both), (single, last)):
                        for part, piece in enumerate(split(val)):
                            at_lane = (part * slots + s) * LANES
                            picked[at, at_lane:at_lane + LANES] = piece
            return c

        lax.fori_loop(0, parts // 2, gather, 0, unroll=UNROLL)
        total = dot(picked[...], jnp.concatenate([weights[...], weights[...]], axis=0))
        total = total[:, :LANES] + total[:, LANES:]
        old = dirn[...]
        left = resid[...] - (old + inv_diag * total)
        resid[...] = left
        new = scal[1 + 2 * i] * old + scal[2 + 2 * i] * left
        dirn[...] = new
        sol[...] = sol[...] + new
        return carry

    lax.fori_loop(0, CHEB, step, 0)
    final = sol[...]
    both = final[:twos].reshape(parts, 2, pairs, LANES)
    a = [both[:, h].reshape(ones, LANES) for h in range(2)]
    out[:, 0] = jnp.where(half, a[0], pltpu.roll(a[1], NP, 1)).reshape(shape)
    out[:, 1] = jnp.where(half, pltpu.roll(a[0], NP, 1), a[1]).reshape(shape)
    out[:, 2] = final[twos:].reshape(shape)


def vmem(n):
    return [pl.BlockSpec(memory_space=pltpu.VMEM)] * n


def shards(velocity, vorticity, blocks, nbr_ref, send_list):
    comps, modes_dev, _, merged = velocity.shape
    n_mode, parts = lax.axis_size("mode"), lax.axis_size("dom")
    slots, elems = nbr_ref.shape
    send = send_list.shape[1]
    pairs = elems // 2
    modes_all = modes_dev * n_mode
    me = lax.axis_index("mode")
    rows = comps * modes_dev * 2

    packed = pl.pallas_call(
        pack_kernel, out_shape=jax.ShapeDtypeStruct((n_mode, 2 * rows, LANES), f32),
        in_specs=[pl.BlockSpec(memory_space=pl.ANY)] * 2, out_specs=vmem(1)[0],
        scratch_shapes=[pltpu.VMEM((2, comps * modes_dev, 2, merged), f32), pltpu.SemaphoreType.DMA((2 * comps,))],
        compiler_params=pltpu.CompilerParams(vmem_limit_bytes=62 << 20), name="pack",
    )(velocity.reshape(comps * modes_dev, 2, merged), vorticity.reshape(comps * modes_dev, 2, merged))
    lines = lax.all_to_all(packed.reshape(n_mode, 1, 2 * rows * LANES), "mode", split_axis=0, concat_axis=0, tiled=True)
    lines = lines.reshape(packed.shape)

    table = jnp.concatenate([
        nbr_ref.reshape(slots, pairs, 2).transpose(1, 2, 0).reshape(pairs, 2 * slots),
        jnp.zeros((pairs, first_send(slots) - 2 * slots), jnp.int32),
        jnp.broadcast_to(send_list.reshape(1, 2 * send), (pairs, 2 * send)),
    ], axis=1).astype(f32)
    table = jnp.pad(table, ((0, 0), (0, LANES - table.shape[1])))
    side = 4
    here = lax.axis_index("dom")
    near = [lax.ppermute(table, "dom", [(d, d // side * side + (d + i) % side) for d in range(parts)])
            for i in range(1, side)]
    table = jnp.stack([table] + near)
    far = [lax.ppermute(table, "dom", [(d, (d + i * side) % parts) for d in range(parts)])
           for i in range(1, parts // side)]
    tables = [table] + far
    steps = jnp.arange(parts, dtype=jnp.int32)
    order = (here // side - steps // side) % (parts // side) * side + (here % side - steps % side) % side
    onehot = pl.pallas_call(
        functools.partial(prep_kernel, parts, pairs, slots, send),
        out_shape=jax.ShapeDtypeStruct((parts // 2, 2 * slots * elems, LANES), bf16),
        in_specs=[pl.BlockSpec(memory_space=pltpu.SMEM)] + vmem(len(tables)), out_specs=vmem(1)[0],
        scratch_shapes=[pltpu.VMEM((parts * pairs, LANES), f32), pltpu.VMEM((parts * pairs, LANES), jnp.int32)],
        compiler_params=pltpu.CompilerParams(vmem_limit_bytes=8 << 20),
        cost_estimate=pl.CostEstimate(flops=0, bytes_accessed=8 << 20, transcendentals=0),
        name="prep",
    )(order, *tables)
    weights = pl.pallas_call(
        functools.partial(weight_kernel, slots),
        out_shape=jax.ShapeDtypeStruct((slots * LANES, 2 * LANES), bf16),
        in_specs=vmem(1), out_specs=vmem(1)[0],
        compiler_params=pltpu.CompilerParams(vmem_limit_bytes=4 << 20),
        cost_estimate=pl.CostEstimate(flops=0, bytes_accessed=1 << 20, transcendentals=0),
        name="weights",
    )(blocks)

    width = comps * LANES
    devices = n_mode * parts
    rhs = pl.pallas_call(
        lines_kernel,
        out_shape=jax.ShapeDtypeStruct((devices, 1, width), f32),
        in_specs=vmem(2), out_specs=vmem(1)[0], name="lines",
        compiler_params=pltpu.CompilerParams(vmem_limit_bytes=12 << 20),
    )(lines, jnp.asarray(spanwise_tables(modes_all, n_mode)))
    mode = me * modes_dev + lax.axis_index("dom") // 2
    wavenum = mode.astype(f32) / modes_all
    coefs = []
    rho = 0.5
    for _ in range(CHEB):
        rho_next = 1.0 / (4.0 - rho)
        coefs += [rho_next * rho, 4.0 * rho_next]
        rho = rho_next
    scal = jnp.concatenate([(1.0 / (1.0 + 4.0 * wavenum * wavenum)).reshape(1), jnp.asarray(coefs, f32)])
    rhs, scal, onehot, weights = lax.optimization_barrier((rhs, scal, onehot, weights))
    columns = lax.all_to_all(rhs, ("dom", "mode"), split_axis=0, concat_axis=0, tiled=True)
    columns = columns.reshape(devices, width)

    rows = parts * pairs * 3
    state = pltpu.VMEM((rows, LANES), f32)
    ext = pltpu.VMEM(((parts + 2) * elems, 4 * LANES), bf16)
    picked = pltpu.VMEM((rows, 2 * slots * LANES), bf16)
    done = pl.pallas_call(
        functools.partial(solve_kernel, parts, pairs, slots),
        out_shape=jax.ShapeDtypeStruct((parts, comps, pairs, LANES), f32),
        in_specs=[pl.BlockSpec(memory_space=pltpu.SMEM)] + vmem(3), out_specs=vmem(1)[0],
        scratch_shapes=[ext, picked, state, state, state],
        compiler_params=pltpu.CompilerParams(
            vmem_limit_bytes=24 << 20),
        name="solve",
    )(scal, columns, onehot, weights)
    back = lax.all_to_all(done.reshape(parts, 1, comps * pairs * LANES), "dom", split_axis=0, concat_axis=0, tiled=True)
    back = back.reshape(modes_dev, 2, comps, pairs, LANES).transpose(2, 0, 1, 3, 4)
    return back.reshape(comps, modes_dev, 2, merged)


def solution(mesh):
    placed = (
        P(None, "mode", None, "dom"),
        P(None, "mode", None, "dom"),
        P(),
        P(None, "dom"),
        P(None, "dom"),
    )
    return jax.shard_map(
        shards, mesh=mesh, in_specs=placed, out_specs=P(None, "mode", None, "dom"), check_vma=False
    )
```
